32 devices in a mesh: cell: 8 (over z, x), lev: 4 (over y, core).
Axes of the slice: x: 2, y: 2, z: 4, core: 2. Of those that a mesh axis runs over, the one named last changes fastest.
Arguments:
- populations: float32 [512, 8192], P('cell', 'lev'), may hold values from 0.5 to 1.5
- rate_blocks: bfloat16 [2, 64, 6, 128, 128], P(None, 'lev'), may hold values from -0.21875 to 0.21875
- pattern: int32 [64, 6], P('lev'), may hold values from 0 to 63, as said below
- bracket: int32 [512], P('cell'), may hold values from 0 to 1
- cross_section: float32 [8192], P('lev'), as said below
- emission: float32 [8192], P('lev'), may hold values from 0.1 to 1
- absorber: float32 [512], P('cell'), as said below
- stream_speed: float32 [512], P('cell'), may hold values from 0.25 to 1
- cross_speed: float32 [512], P('cell'), may hold values from -1 to 1
- inflow: float32 [16, 8192], P(None, 'lev'), may hold values from 0.5 to 1.5
Outputs:
- updated: float32 [512, 8192], P('cell', 'lev')
- absorption: float32 [512, 8192], P('cell', 'lev')
The draws below stay inside these ranges and needn't reach their ends.
Inputs may be any that keep to these rules, and one draw needn't show every extreme that they name: Row r of pattern lists 6 distinct level blocks, the first of them r itself. `cross_section`: each cross section lies between 0.1 / 32 and 0.035. `absorber`: absorber columns lie between 0.5 and 2, except a few whole streamwise rows where they equal 48.
All inputs are finite; a program needn't handle non-finite values.
Results may differ from the reference program's by a relative error of at most 0.00055.
Values may be sent and summed in bfloat16 or wider, within the bound.
A program may use at most 128 MiB of HBM per device.

```python
import math
import jax
import jax.numpy as jnp
from jax import lax

LEVELS = 8192
BLOCK = 128
NZB = 6
NBR = 2
NY = 16
NBLOCKS = 64
STREAMWISE_NUM = 32
CELLS = 512


def draw_pattern(key, part):
    block_count = LEVELS // BLOCK
    row_keys = jax.random.split(jax.random.fold_in(key, 3), block_count)

    def one_row(row_key, row_index):
        shuffled = jax.random.permutation(row_key, block_count - 1)[:NZB - 1]
        others = (row_index + 1 + shuffled) % block_count
        return jnp.concatenate([row_index[None], others]).astype(jnp.int32)
    return jax.vmap(one_row)(row_keys, jnp.arange(block_count, dtype=jnp.int32))


def draw_cross_section(key, part):
    key_pick, key_fast, key_slow = jax.random.split(jax.random.fold_in(key, 5), 3)
    fast_share = 0.5
    is_fast = jax.random.uniform(key_pick, (LEVELS,)) < fast_share
    fast_value = jnp.exp(jax.random.uniform(key_fast, (LEVELS,), minval=math.log(0.02), maxval=math.log(0.035)))
    slow_value = jnp.exp(jax.random.uniform(key_slow, (LEVELS,), minval=math.log(0.1), maxval=math.log(0.3))) / STREAMWISE_NUM
    return jnp.where(is_fast, fast_value, slow_value).astype(jnp.float32)


def draw_absorber(key, part):
    key_background, key_pulse = jax.random.split(jax.random.fold_in(key, 9))
    baseline_level = jnp.exp(jax.random.uniform(key_background, (STREAMWISE_NUM, NY), minval=math.log(0.5), maxval=math.log(2.0)))
    pulse_rows = jax.random.randint(key_pulse, (3,), 0, STREAMWISE_NUM)
    inside_pulse = jnp.any(jnp.arange(STREAMWISE_NUM)[:, None] == pulse_rows[None, :], axis=1)
    number_density = jnp.where(inside_pulse[:, None], 1.5 * STREAMWISE_NUM, baseline_level)
    return number_density.reshape(STREAMWISE_NUM * NY).astype(jnp.float32)


def place_ends(values, rng, least, high):
    extent = values.shape
    place = [jax.random.randint(jax.random.fold_in(rng, axis), (), 0, extent[axis]) for axis in range(len(extent))]
    values = values.at[tuple(place)].set(least)
    longest = extent.index(max(extent))
    place[longest] = (place[longest] + 1) % extent[longest]
    return values.at[tuple(place)].set(high)


def shard_levels(rng, dims, shards, least, largest):
    def one(dim, parts):
        steps = jax.random.uniform(jax.random.fold_in(jax.random.fold_in(rng, 6), dim), (parts,), jnp.float32, least / len(shards), largest / len(shards))
        return jnp.repeat(jnp.exp(steps), dims[dim] // parts).reshape((-1,) + (1,) * (len(dims) - dim - 1))

    factor_of = one(*shards[0])
    for cut in shards[1:]:
        factor_of = factor_of * one(*cut)
    return factor_of


def scatter_about(rng, dims, spread, limit, cuts=(), kind=jnp.bfloat16):
    result = jax.random.normal(rng, dims, jnp.float32) * spread
    if len(cuts) > 0:
        result = shard_levels(rng, dims, cuts, -0.22, 0.18) * result
    return jnp.clip(result, min=-limit, max=limit).astype(kind)


def setup_inputs(seed: int = 0) -> dict:
    key_of = jax.random.split(jax.random.key(seed), 11)
    populations = jnp.clip(0.5 + 1.0 * jax.random.uniform(key_of[0], (CELLS, LEVELS), jnp.float32) ** shard_levels(key_of[0], (CELLS, LEVELS), ((0, 8), (1, 4)), -0.2, 0.2), 0.5, 1.5)
    rate_blocks = scatter_about(key_of[1], (NBR, NBLOCKS, NZB, BLOCK, BLOCK), (NZB * BLOCK) ** -0.5, 0.21875, ((1, 4),))
    pattern = draw_pattern(jax.random.fold_in(key_of[10], 71), 0)
    bracket = place_ends(jax.random.randint(key_of[3], (CELLS,), 0, NBR), jax.random.fold_in(key_of[3], 1), 0, NBR - 1).astype(jnp.int32)
    cross_section = draw_cross_section(jax.random.fold_in(key_of[10], 71), 0)
    emission = jnp.clip(jnp.exp(math.log(1.0) - 2.3025851 * jax.random.uniform(key_of[5], (LEVELS,), jnp.float32) ** shard_levels(key_of[5], (LEVELS,), ((0, 4),), -0.2, 0.2)), 0.1, 1.0)
    absorber = draw_absorber(jax.random.fold_in(key_of[10], 71), 0)
    stream_speed = jnp.clip(0.25 + 0.75 * jax.random.uniform(key_of[7], (CELLS,), jnp.float32) ** shard_levels(key_of[7], (CELLS,), ((0, 8),), -0.2, 0.2), 0.25, 1.0)
    cross_speed = jnp.clip(jax.random.uniform(key_of[8], (CELLS,), jnp.float32, -1.0, 1.0) * shard_levels(key_of[8], (CELLS,), ((0, 8),), -0.4, 0.0), -1.0, 1.0)
    inflow = jnp.clip(0.5 + 1.0 * jax.random.uniform(key_of[9], (NY, LEVELS), jnp.float32) ** shard_levels(key_of[9], (NY, LEVELS), ((1, 4),), -0.2, 0.2), 0.5, 1.5)
    return {"populations": populations, "rate_blocks": rate_blocks, "pattern": pattern, "bracket": bracket, "cross_section": cross_section, "emission": emission, "absorber": absorber, "stream_speed": stream_speed, "cross_speed": cross_speed, "inflow": inflow}


time_step = 0.25


def rate_term(populations, rate_blocks, pattern, bracket):
    lowered = lax.optimization_barrier(populations.astype(jnp.bfloat16)).astype(jnp.float32)
    blocks_all = lowered.reshape(CELLS, NBLOCKS, BLOCK)

    def one_row(row_block):
        columns = blocks_all[:, pattern[row_block], :]
        summed = jnp.zeros((CELLS, BLOCK), jnp.float32)
        for bracket_id in range(NBR):
            table = rate_blocks[bracket_id, row_block].astype(jnp.float32)
            product = jnp.einsum("ckj,kij->ci", columns, table)
            summed = jnp.where((bracket == bracket_id)[:, None], product, summed)
        return summed

    stacked = lax.map(one_row, jnp.arange(NBLOCKS, dtype=jnp.int32))
    return jnp.transpose(stacked, (1, 0, 2)).reshape(CELLS, LEVELS)


def radiation(populations, emission, cross_section, absorber):
    emitted = populations * emission[None, :]
    transmit = jnp.exp(-(absorber[:, None] * cross_section[None, :]))
    layered_pass = transmit.reshape(STREAMWISE_NUM, NY, LEVELS)
    layered_emit = emitted.reshape(STREAMWISE_NUM, NY, LEVELS)

    def advance(running, layer_in):
        transmit_x, source_x = layer_in
        renewed = transmit_x * running + source_x
        return renewed, renewed

    nothing = jnp.zeros((NY, LEVELS), jnp.float32)
    _, downward = lax.scan(advance, nothing, (layered_pass, layered_emit))
    _, upward = lax.scan(advance, nothing, (layered_pass, layered_emit), reverse=True)
    absorbed = (1.0 - layered_pass) * (downward + upward - 2.0 * layered_emit)
    return emitted, absorbed.reshape(CELLS, LEVELS)


def advection(populations, inflow, stream_speed, cross_speed):
    layered = populations.reshape(STREAMWISE_NUM, NY, LEVELS)
    upstream = jnp.concatenate([inflow[None], layered[:-1]], axis=0)
    before_y = jnp.roll(layered, 1, axis=1)
    after_y = jnp.roll(layered, -1, axis=1)
    along_x = stream_speed.reshape(STREAMWISE_NUM, NY, 1)
    along_y = cross_speed.reshape(STREAMWISE_NUM, NY, 1)
    flux_sum = -along_x * (layered - upstream) - jnp.maximum(along_y, 0.0) * (layered - before_y) - jnp.minimum(along_y, 0.0) * (after_y - layered)
    return flux_sum.reshape(CELLS, LEVELS)


def tendency(populations, rate_blocks, pattern, bracket, cross_section, emission, absorber, stream_speed, cross_speed, inflow):
    rates_part = rate_term(populations, rate_blocks, pattern, bracket)
    emitted, absorbed = radiation(populations, emission, cross_section, absorber)
    carried = advection(populations, inflow, stream_speed, cross_speed)
    return rates_part - emitted + absorbed + carried, absorbed


def reference(populations, rate_blocks, pattern, bracket, cross_section, emission, absorber, stream_speed, cross_speed, inflow):
    first_rate, _ = tendency(populations, rate_blocks, pattern, bracket, cross_section, emission, absorber, stream_speed, cross_speed, inflow)
    middle = populations + time_step * first_rate
    second, absorption = tendency(middle, rate_blocks, pattern, bracket, cross_section, emission, absorber, stream_speed, cross_speed, inflow)
    updated = 0.5 * (populations + middle + time_step * second)
    return (updated, absorption)
```

```python
import functools

import jax
import jax.numpy as jnp
from jax import lax
from jax.experimental import pallas as pl
from jax.experimental.pallas import tpu as pltpu
from jax.sharding import PartitionSpec as P

NY = 16
LANES = 128

time_step = 0.25

MESH = pl.DeviceIdType.MESH


def fused_kernel(
    strips,
    groups,
    pattern_hbm,
    p_hbm,
    rates_hbm,
    bracket_hbm,
    absorber_hbm,
    stream_hbm,
    turn_hbm,
    cross_hbm,
    emission_hbm,
    inflow_hbm,
    advanced_ref,
    gained_ref,
    pattern_ref,
    p_ref,
    bracket_ref,
    absorber_ref,
    stream_ref,
    turn_ref,
    cross_ref,
    emission_ref,
    inflow_ref,
    rates,
    coef,
    passing,
    middle,
    rate_sum,
    gathered_first,
    gathered_second,
    halo,
    columns,
    share_pass,
    out_one,
    in_one,
    out_two,
    in_two,
    rates_sem,
    operand_sem,
    gather_send,
    gather_recv,
    forward_send,
    halo_send,
    halo_recv,
    column_send,
    column_recv,
    one_send,
    one_recv,
    two_send,
    two_recv,
):
    cell = lax.axis_index("cell")
    gathered = (gathered_first, gathered_second)
    lev = lax.axis_index("lev")
    cell_count = p_ref.shape[0]
    layers = cell_count // NY
    blocks = p_ref.shape[1] // LANES
    per_owner = blocks // strips
    brackets, _, nonzero = rates_hbm.shape[:3]
    partner = lev + 1 - 2 * lax.rem(lev, 2)

    operands = [
        pltpu.make_async_copy(source, into, operand_sem.at[index])
        for index, (source, into) in enumerate(
            (
                (p_hbm, p_ref),
                (absorber_hbm, absorber_ref),
                (cross_hbm, cross_ref),
                (emission_hbm, emission_ref),
                (stream_hbm, stream_ref),
                (turn_hbm, turn_ref),
                (bracket_hbm, bracket_ref),
                (inflow_hbm, inflow_ref),
                (pattern_hbm, pattern_ref),
            )
        )
    ]
    for copy in operands:
        copy.start()
    fetch = pltpu.make_async_copy(rates_hbm, rates, rates_sem)
    fetch.start()

    barrier = pltpu.get_barrier_semaphore()
    greeted = 0
    for step in range(1, strips):
        pl.semaphore_signal(
            barrier,
            inc=1,
            device_id={"cell": lax.rem(cell + step, strips), "lev": lev},
            device_id_type=MESH,
        )
        greeted += 1
    for step in range(1, groups // 2):
        pl.semaphore_signal(
            barrier,
            inc=1,
            device_id={"cell": cell, "lev": lax.rem(lev + 2 * step, groups)},
            device_id_type=MESH,
        )
        greeted += 1
    pl.semaphore_signal(barrier, inc=1, device_id={"cell": cell, "lev": partner}, device_id_type=MESH)
    greeted += 1

    def rows(x):
        return slice(x * NY, (x + 1) * NY)

    def spread(row):
        shape = (cell_count, cell_count)
        here = lax.broadcasted_iota(jnp.int32, shape, 0) == lax.broadcasted_iota(jnp.int32, shape, 1)
        column = jnp.sum(jnp.where(here, row, 0.0), axis=1, keepdims=True)
        return jnp.broadcast_to(column, (cell_count, LANES))

    def summed_layers(row):
        shape = (NY, cell_count)
        cell_y = lax.rem(lax.broadcasted_iota(jnp.int32, shape, 1), NY)
        here = lax.broadcasted_iota(jnp.int32, shape, 0) == cell_y
        column = jnp.sum(jnp.where(here, row, 0.0), axis=1, keepdims=True)
        return jnp.broadcast_to(column, (NY, LANES))

    def lanes(block):
        return pl.ds(pl.multiple_of(block * LANES, LANES), LANES)

    chunks = gather_recv.shape[2]
    piece = blocks // chunks

    def own_slot(part, who, chunk):
        return gathered[part].at[pl.ds(who * blocks + chunk * piece, piece)]

    def gather_copy(part, to, source, send_sem, chunk):
        return pltpu.make_async_remote_copy(
            src_ref=own_slot(part, source, chunk),
            dst_ref=own_slot(part, source, chunk),
            send_sem=send_sem.at[chunk],
            recv_sem=gather_recv.at[part, source, chunk],
            device_id={"cell": cell, "lev": to},
            device_id_type=MESH,
        )

    def halo_copy(part):
        return pltpu.make_async_remote_copy(
            src_ref=gathered[part].at[pl.ds(lev * blocks, blocks), pl.ds(cell_count - NY, NY)],
            dst_ref=halo.at[part],
            send_sem=halo_send.at[part],
            recv_sem=halo_recv.at[part],
            device_id={"cell": lax.rem(cell + 1, strips), "lev": lev},
            device_id_type=MESH,
        )

    def column_copy(step):
        to = lax.rem(cell + step, strips)
        return pltpu.make_async_remote_copy(
            src_ref=columns.at[cell],
            dst_ref=columns.at[cell],
            send_sem=column_send.at[step],
            recv_sem=column_recv.at[step],
            device_id={"cell": to, "lev": lev},
            device_id_type=MESH,
        )

    def strip_copy(part, step, out, into, send_sem, recv_sem):
        to = lax.rem(cell + step, strips)
        return pltpu.make_async_remote_copy(
            src_ref=out.at[part, to],
            dst_ref=into.at[part, cell],
            send_sem=send_sem.at[part, step],
            recv_sem=recv_sem.at[part, step],
            device_id={"cell": to, "lev": lev},
            device_id_type=MESH,
        )

    def emitted_of(value, block):
        return value * emission_ref[pl.ds(block, 1), :]

    def put(ref, part, index, downs, ups):
        means = []
        for place, value in enumerate(downs + ups):
            mean = jnp.mean(value, axis=0, keepdims=True).astype(jnp.bfloat16).astype(jnp.float32)
            ref[part, index, place] = (value - mean).astype(jnp.bfloat16)
            means.append(mean)
        means.append(jnp.zeros((NY - len(means), LANES), jnp.float32))
        ref[part, index, 2 * per_owner] = jnp.concatenate(means, axis=0).astype(jnp.bfloat16)

    def get(ref, part, index, b):
        means = ref[part, index, 2 * per_owner].astype(jnp.float32)
        return tuple(
            ref[part, index, place].astype(jnp.float32) + means[place : place + 1]
            for place in (b, per_owner + b)
        )

    def lower(part, block, value):
        gathered[part][lev * blocks + block] = value.astype(jnp.bfloat16)

    def summarize(part, owner, values):
        downs, ups = [], []
        for b in range(per_owner):
            block = owner * per_owner + b
            through = [passing[block, rows(x), :] for x in range(layers)]
            emit = [emitted_of(values[b][x], block) for x in range(layers)]
            down, up = emit[0], emit[-1]
            for x in range(1, layers):
                down = through[x] * down + emit[x]
                up = through[layers - 1 - x] * up + emit[layers - 1 - x]
            downs.append(down)
            ups.append(up)
        put(out_one, part, owner, downs, ups)

    def load_start(block):
        return [p_ref[rows(x), lanes(block)] for x in range(layers)]

    def start_gather(part, chunk):
        for step in range(1, groups // 2):
            to = lax.rem(lev + 2 * step, groups)
            gather_copy(part, to, lev, gather_send.at[part, step], chunk).start()
        gather_copy(part, partner, lev, gather_send.at[part, 0], chunk).start()

    def start_halo(part):
        @pl.when(cell < strips - 1)
        def _():
            halo_copy(part).start()

    def lower_start(block, _):
        lower(0, block, p_ref[:, lanes(block)])
        return 0

    operands[0].wait()
    operands[1].wait()
    columns[cell] = absorber_ref[...]
    pl.semaphore_wait(barrier, greeted)
    for chunk in range(chunks):
        lax.fori_loop(chunk * piece, (chunk + 1) * piece, lower_start, 0, unroll=2)
        start_gather(0, chunk)
    for step in range(1, strips):
        column_copy(step).start()

    for copy in operands[2:]:
        copy.wait()
    coef[0] = spread(absorber_ref[...])

    def pass_block(block, _):
        passing[block] = jnp.exp(-(coef[0] * cross_ref[pl.ds(block, 1), :]))
        return 0

    def summarize_start(owner, _):
        values = []
        for b in range(per_owner):
            pass_block(owner * per_owner + b, 0)
            values.append(load_start(owner * per_owner + b))
        summarize(0, owner, values)
        return 0

    lax.fori_loop(0, strips, summarize_start, 0)

    def start_one(part):
        for step in range(1, strips):
            strip_copy(part, step, out_one, in_one, one_send, one_recv).start()
        in_one[part, cell] = out_one[part, cell]

    start_one(0)
    start_halo(0)
    coef[1] = spread(stream_ref[...])
    coef[2] = spread(turn_ref[...])
    coef[3] = spread(bracket_ref[...].astype(jnp.float32))
    for step in range(1, strips):
        column_copy(step).wait()

    def share_block(strip, _):
        column = summed_layers(columns[strip])
        for b in range(per_owner):
            cross = cross_ref[pl.ds(cell * per_owner + b, 1), :]
            share_pass[strip, b] = jnp.exp(-(column * cross))
        return 0

    lax.fori_loop(0, strips, share_block, 0)

    def enter(part):
        for step in range(1, strips):
            strip_copy(part, step, out_one, in_one, one_send, one_recv).wait()
        below = [[] for _ in range(strips)]
        above = [[] for _ in range(strips)]
        for b in range(per_owner):
            parts = [get(in_one, part, strip, b) for strip in range(strips)]
            running = jnp.zeros((NY, LANES), jnp.float32)
            for strip in range(strips):
                below[strip].append(running)
                running = share_pass[strip, b] * running + parts[strip][0]
            running = jnp.zeros((NY, LANES), jnp.float32)
            for strip in reversed(range(strips)):
                above[strip].append(running)
                running = share_pass[strip, b] * running + parts[strip][1]
        for strip in range(strips):
            put(out_two, part, strip, below[strip], above[strip])
        for step in range(1, strips):
            strip_copy(part, step, out_two, in_two, two_send, two_recv).start()
        in_two[part, cell] = out_two[part, cell]

    def forward(part, chunk):
        for step in range(1, groups // 2):
            source = lax.rem(lev + 2 * step, groups)
            gather_copy(part, lev, source, gather_send.at[part, step], chunk).wait_recv()
            gather_copy(part, partner, source, forward_send.at[part, step], chunk).start()

    def rates_of(part):
        for chunk in range(chunks):
            gather_copy(part, partner, partner, gather_send.at[part, 0], chunk).wait_recv()
            for step in range(1, groups // 2):
                source = lax.rem(partner + 2 * step, groups)
                gather_copy(part, lev, source, gather_send.at[part, step], chunk).wait_recv()

        def one_row(row, _):
            picked = jnp.concatenate(
                [gathered[part][pattern_ref[k, row]] for k in range(nonzero)], axis=1
            )
            table = jnp.concatenate(
                [
                    jnp.concatenate([rates[bracket, row, k] for k in range(nonzero)], axis=1)
                    for bracket in range(brackets)
                ],
                axis=0,
            )
            product = lax.dot_general(
                picked, table, (((1,), (1,)), ((), ())), preferred_element_type=jnp.float32
            )
            kind = coef[3]
            summed = product[:, :LANES]
            for bracket in range(1, brackets):
                summed = jnp.where(
                    kind == float(bracket),
                    product[:, bracket * LANES : (bracket + 1) * LANES],
                    summed,
                )
            rate_sum[row] = summed
            return 0

        lax.fori_loop(0, blocks, one_row, 0, unroll=4)

    def finish_transfers(part):
        for chunk in range(chunks):
            for step in range(1, groups // 2):
                gather_copy(part, partner, lev, gather_send.at[part, step], chunk).wait_send()
                gather_copy(part, partner, lev, forward_send.at[part, step], chunk).wait_send()
            gather_copy(part, partner, lev, gather_send.at[part, 0], chunk).wait_send()

        @pl.when(cell < strips - 1)
        def _():
            halo_copy(part).wait_send()

    def before_close(part):
        @pl.when(cell > 0)
        def _():
            halo_copy(part).wait_recv()

        @pl.when(cell == 0)
        def _():
            for block in range(blocks):
                halo[part, block] = inflow_ref[:, block * LANES : (block + 1) * LANES].astype(
                    jnp.bfloat16
                )

        for step in range(1, strips):
            strip_copy(part, step, out_two, in_two, two_send, two_recv).wait()

    def tendency(part, owner, b, value):
        block = owner * per_owner + b
        through = [passing[block, rows(x), :] for x in range(layers)]
        emit = [emitted_of(value[x], block) for x in range(layers)]
        down, up = get(in_two, part, owner, b)
        downs, ups = [None] * layers, [None] * layers
        for x in range(layers):
            down = through[x] * down + emit[x]
            downs[x] = down
            back = layers - 1 - x
            up = through[back] * up + emit[back]
            ups[back] = up
        arrived = halo[part, block].astype(jnp.float32)
        entering = jnp.where(cell == 0, inflow_ref[:, lanes(block)], arrived)
        gains, total = [], []
        for x in range(layers):
            gained = downs[x] + ups[x] - 2.0 * emit[x]
            taken = (1.0 - through[x]) * gained
            upstream = entering if x == 0 else value[x - 1]
            before_y = pltpu.roll(value[x], 1, 0)
            after_y = pltpu.roll(value[x], NY - 1, 0)
            cross = coef[2, rows(x), :]
            carried = (
                -coef[1, rows(x), :] * (value[x] - upstream)
                - jnp.maximum(cross, 0.0) * (value[x] - before_y)
                - jnp.minimum(cross, 0.0) * (after_y - value[x])
            )
            gains.append(gained)
            total.append(rate_sum[block, rows(x), :] - emit[x] + taken + carried)
        return gains, total

    def exchange(part):
        for chunk in range(chunks - 1):
            forward(part, chunk)
        enter(part)
        forward(part, chunks - 1)

    exchange(0)
    fetch.wait()
    rates_of(0)
    before_close(0)

    def close_first(owner, _):
        values = []
        for b in range(per_owner):
            block = owner * per_owner + b
            value = load_start(block)
            _, total = tendency(0, owner, b, value)
            renewed = [value[x] + time_step * total[x] for x in range(layers)]
            for x in range(layers):
                middle[block, rows(x), :] = renewed[x]
            lower(1, block, jnp.concatenate(renewed, axis=0))
            values.append(renewed)
        summarize(1, owner, values)
        return 0

    owners = strips // chunks
    for chunk in range(chunks):
        lax.fori_loop(chunk * owners, (chunk + 1) * owners, close_first, 0)
        start_gather(1, chunk)
    start_one(1)
    start_halo(1)
    finish_transfers(0)
    exchange(1)
    rates_of(1)
    before_close(1)

    def close_second(owner, _):
        for b in range(per_owner):
            block = owner * per_owner + b
            value = [middle[block, rows(x), :] for x in range(layers)]
            gains, total = tendency(1, owner, b, value)
            for x in range(layers):
                gained_ref[rows(x), lanes(block)] = gains[x]
                advanced_ref[rows(x), lanes(block)] = value[x] + time_step * total[x]
        return 0

    lax.fori_loop(0, strips, close_second, 0)
    finish_transfers(1)


def fused(
    strips,
    groups,
    populations,
    rate_blocks,
    pattern,
    bracket,
    cross_section,
    emission,
    absorber,
    stream_speed,
    cross_speed,
    inflow,
):
    cell_count, level_count = populations.shape
    blocks = level_count // LANES
    per_owner = blocks // strips
    chunks = 4 if strips % 4 == 0 else 1
    layers_shape = (blocks, cell_count, LANES)
    share = (2, strips, 2 * per_owner + 1, NY, LANES)
    vmem = pl.BlockSpec(memory_space=pltpu.VMEM)
    dma = pltpu.SemaphoreType.DMA
    operands = [
        pattern.T,
        populations,
        rate_blocks,
        bracket.reshape(1, -1),
        absorber.reshape(1, -1),
        stream_speed.reshape(1, -1),
        cross_speed.reshape(1, -1),
        cross_section.reshape(blocks, LANES),
        emission.reshape(blocks, LANES),
        inflow,
    ]
    held = [pltpu.VMEM(value.shape, value.dtype) for value in operands]
    held[0] = pltpu.SMEM(operands[0].shape, operands[0].dtype)
    del held[2]
    return pl.pallas_call(
        functools.partial(fused_kernel, strips, groups),
        out_shape=[pltpu.VMEM((cell_count, level_count), jnp.float32)] * 2,
        in_specs=[pl.BlockSpec(memory_space=pltpu.HBM)] * len(operands),
        out_specs=[vmem, vmem],
        scratch_shapes=held
        + [
            pltpu.VMEM(rate_blocks.shape, rate_blocks.dtype),
            pltpu.VMEM((4, cell_count, LANES), jnp.float32),
            pltpu.VMEM(layers_shape, jnp.float32),
            pltpu.VMEM(layers_shape, jnp.float32),
            pltpu.VMEM(layers_shape, jnp.float32),
            pltpu.VMEM((groups * blocks, cell_count, LANES), jnp.bfloat16),
            pltpu.VMEM((groups * blocks, cell_count, LANES), jnp.bfloat16),
            pltpu.VMEM((2, blocks, NY, LANES), jnp.bfloat16),
            pltpu.VMEM((strips, 1, cell_count), jnp.float32),
            pltpu.VMEM((strips, per_owner, NY, LANES), jnp.float32),
            pltpu.VMEM(share, jnp.bfloat16),
            pltpu.VMEM(share, jnp.bfloat16),
            pltpu.VMEM(share, jnp.bfloat16),
            pltpu.VMEM(share, jnp.bfloat16),
            dma(()),
            dma((len(held),)),
            dma((2, groups, chunks)),
            dma((2, groups, chunks)),
            dma((2, groups, chunks)),
            dma((2,)),
            dma((2,)),
            dma((strips,)),
            dma((strips,)),
            dma((2, strips)),
            dma((2, strips)),
            dma((2, strips)),
            dma((2, strips)),
        ],
        compiler_params=pltpu.CompilerParams(
            collective_id=0, has_side_effects=True, vmem_limit_bytes=24 * 1024 * 1024
        ),
    )(*[pltpu.with_memory_space_constraint(value, pltpu.HBM) for value in operands])


def shortened(value):

    def short(part):
        return part.astype(jnp.bfloat16) if part.dtype == jnp.float32 else part

    return jax.tree.map(short, value)


def shifted(value, axis, by):
    peers = lax.axis_size(axis)
    pairs = [(i, i + by) for i in range(peers) if 0 <= i + by < peers]
    return lax.ppermute(value, axis, pairs)


def affine(earlier, later):
    return (earlier[0] * later[0], later[0] * earlier[1] + later[1])


def rate_term(populations, rate_blocks, pattern, bracket):
    lowered = populations.astype(jnp.bfloat16)
    gathered = lax.all_gather(lowered, "lev", axis=1, tiled=True)
    cell_count = gathered.shape[0]
    brackets, rows, nonzero, block_size = rate_blocks.shape[:4]
    by_block = jnp.swapaxes(gathered.reshape(cell_count, -1, block_size), 0, 1)

    def one_row(row):
        summed = jnp.zeros((cell_count, block_size), jnp.float32)
        for bracket_id in range(brackets):
            product = jnp.zeros((cell_count, block_size), jnp.float32)
            for k in range(nonzero):
                column = lax.dynamic_index_in_dim(by_block, pattern[row, k], 0, keepdims=False)
                table = lax.dynamic_index_in_dim(rate_blocks[bracket_id], row, 0, keepdims=False)[k]
                product += jnp.einsum("cj,ij->ci", column, table, preferred_element_type=jnp.float32)
            summed = jnp.where((bracket == bracket_id)[:, None], product, summed)
        return summed

    stacked = lax.map(one_row, jnp.arange(rows, dtype=jnp.int32))
    return jnp.transpose(stacked, (1, 0, 2)).reshape(cell_count, -1)


def entering(received):
    start = jnp.zeros(received.shape[2:], jnp.float32)

    def advance(running, layer_in):
        return (layer_in[0] * running + layer_in[1], running)

    _, from_below = lax.scan(advance, start, (received[:, 0], received[:, 1]))
    _, from_above = lax.scan(advance, start, (received[:, 2], received[:, 3]), reverse=True)
    both_sides = jnp.stack([from_below, from_above], axis=1)
    return lax.all_to_all(both_sides, "cell", split_axis=0, concat_axis=3, tiled=True)


def radiation(populations, emission, cross_section, absorber):
    cell_count, level_count = populations.shape
    strips = cell_count // NY
    emitted = populations * emission[None, :]
    transmit = jnp.exp(-(absorber[:, None] * cross_section[None, :]))
    layered_pass = transmit.reshape(strips, NY, level_count)
    layered_emit = emitted.reshape(strips, NY, level_count)
    passed_down, local_down = lax.associative_scan(affine, (layered_pass, layered_emit), axis=0)
    passed_up, local_up = lax.associative_scan(
        affine, (layered_pass, layered_emit), reverse=True, axis=0
    )
    summary = jnp.stack([passed_down[-1], local_down[-1], passed_up[0], local_up[0]])[None]
    returned = entering(lax.all_to_all(summary, "cell", split_axis=3, concat_axis=0, tiled=True))
    enter_down = returned[0, 0]
    enter_up = returned[0, 1]
    downward = local_down + passed_down * enter_down[None]
    upward = local_up + passed_up * enter_up[None]
    absorbed = (1.0 - layered_pass) * (downward + upward - 2.0 * layered_emit)
    return (emitted, absorbed.reshape(cell_count, level_count))


def advection(populations, inflow, stream_speed, cross_speed):
    cell_count, level_count = populations.shape
    layered = populations.reshape(cell_count // NY, NY, level_count)
    arrived = shifted(shortened(layered[-1]), "cell", 1)
    boundary = jnp.where(lax.axis_index("cell") == 0, inflow, arrived)
    upstream = jnp.concatenate([boundary[None], layered[:-1]], axis=0)
    before_y = jnp.roll(layered, 1, axis=1)
    after_y = jnp.roll(layered, -1, axis=1)
    along_x = stream_speed.reshape(-1, NY, 1)
    along_y = cross_speed.reshape(-1, NY, 1)
    flux_sum = (
        -along_x * (layered - upstream)
        - jnp.maximum(along_y, 0.0) * (layered - before_y)
        - jnp.minimum(along_y, 0.0) * (after_y - layered)
    )
    return flux_sum.reshape(cell_count, level_count)


def tendency(
    populations,
    rate_blocks,
    pattern,
    bracket,
    cross_section,
    emission,
    absorber,
    stream_speed,
    cross_speed,
    inflow,
):
    rates_part = rate_term(populations, rate_blocks, pattern, bracket)
    emitted, absorbed = radiation(populations, emission, cross_section, absorber)
    carried = advection(populations, inflow, stream_speed, cross_speed)
    return (rates_part - emitted + absorbed + carried, absorbed)


def local(
    populations,
    rate_blocks,
    pattern,
    bracket,
    cross_section,
    emission,
    absorber,
    stream_speed,
    cross_speed,
    inflow,
):
    strips, groups = lax.axis_size("cell"), lax.axis_size("lev")
    cell_count, level_count = populations.shape
    if (
        groups % 2 == 0
        and strips > 1
        and cell_count % NY == 0
        and level_count % (strips * LANES) == 0
        and rate_blocks.shape[3] == LANES
        and 2 * level_count <= strips * LANES * NY
    ):
        advanced, gained = (
            fused(
                strips,
                groups,
                populations,
                rate_blocks,
                pattern,
                bracket,
                cross_section,
                emission,
                absorber,
                stream_speed,
                cross_speed,
                inflow,
            )
        )
        transmit = jnp.exp(-(absorber[:, None] * cross_section[None, :]))
        return (0.5 * (populations + advanced), (1.0 - transmit) * gained)
    first_rate, _ = tendency(
        populations,
        rate_blocks,
        pattern,
        bracket,
        cross_section,
        emission,
        absorber,
        stream_speed,
        cross_speed,
        inflow,
    )
    middle = populations + time_step * first_rate
    second, absorption = tendency(
        middle,
        rate_blocks,
        pattern,
        bracket,
        cross_section,
        emission,
        absorber,
        stream_speed,
        cross_speed,
        inflow,
    )
    updated = 0.5 * (populations + middle + time_step * second)
    return (updated, absorption)


def solution(mesh):
    in_specs = (
        P("cell", "lev"),
        P(None, "lev", None, None, None),
        P("lev", None),
        P("cell"),
        P("lev"),
        P("lev"),
        P("cell"),
        P("cell"),
        P("cell"),
        P(None, "lev"),
    )
    out_specs = (P("cell", "lev"), P("cell", "lev"))
    return jax.shard_map(local, mesh=mesh, in_specs=in_specs, out_specs=out_specs, check_vma=False)
```

```python
import functools

import jax
import jax.numpy as jnp
from jax import lax
from jax.experimental import pallas as pl
from jax.experimental.pallas import tpu as pltpu
from jax.sharding import PartitionSpec as P

NY = 16
LANES = 128

time_step = 0.25

MESH = pl.DeviceIdType.MESH


def fused_kernel(
    strips,
    groups,
    pattern_hbm,
    p_hbm,
    rates_hbm,
    bracket_hbm,
    absorber_hbm,
    stream_hbm,
    turn_hbm,
    cross_hbm,
    emission_hbm,
    inflow_hbm,
    advanced_ref,
    gained_ref,
    pattern_ref,
    p_ref,
    bracket_ref,
    absorber_ref,
    stream_ref,
    turn_ref,
    cross_ref,
    emission_ref,
    inflow_ref,
    rates,
    coef,
    passing,
    middle,
    gathered_first,
    gathered_second,
    halo,
    columns,
    near_pass,
    far_pass,
    out_one,
    in_near,
    in_far,
    out_two,
    in_two,
    rates_sem,
    operand_sem,
    gather_send,
    gather_recv,
    forward_send,
    partner_send,
    partner_recv,
    halo_send,
    halo_recv,
    column_send,
    column_recv,
    near_send,
    near_recv,
    far_send,
    far_recv,
    two_send,
    two_recv,
):
    cell = lax.axis_index("cell")
    lev = lax.axis_index("lev")
    gathered = (gathered_first, gathered_second)
    cell_count = p_ref.shape[0]
    layers = cell_count // NY
    blocks = p_ref.shape[1] // LANES
    half = strips // 2
    piece = blocks // half
    brackets, _, nonzero = rates_hbm.shape[:3]
    partner = lev + 1 - 2 * lax.rem(lev, 2)
    side = cell // half
    pos = lax.rem(cell, half)
    base = side * half
    other = (1 - side) * half
    slot = pos + side * (half - 1 - 2 * pos)

    barrier = pltpu.get_barrier_semaphore()
    greeted = 0
    for step in range(1, strips):
        pl.semaphore_signal(
            barrier,
            inc=1,
            device_id={"cell": lax.rem(cell + step, strips), "lev": lev},
            device_id_type=MESH,
        )
        greeted += 1
    for step in range(1, groups // 2):
        pl.semaphore_signal(
            barrier,
            inc=1,
            device_id={"cell": cell, "lev": lax.rem(lev + 2 * step, groups)},
            device_id_type=MESH,
        )
        greeted += 1
    pl.semaphore_signal(barrier, inc=1, device_id={"cell": cell, "lev": partner}, device_id_type=MESH)
    greeted += 1

    operands = [
        pltpu.make_async_copy(source, into, operand_sem.at[index])
        for index, (source, into) in enumerate(
            (
                (p_hbm, p_ref),
                (absorber_hbm, absorber_ref),
                (cross_hbm, cross_ref),
                (emission_hbm, emission_ref),
                (stream_hbm, stream_ref),
                (turn_hbm, turn_ref),
                (bracket_hbm, bracket_ref),
                (inflow_hbm, inflow_ref),
                (pattern_hbm, pattern_ref),
            )
        )
    ]
    for copy in operands:
        copy.start()
    fetch = pltpu.make_async_copy(rates_hbm, rates, rates_sem)
    fetch.start()

    def rows(x):
        return slice(x * NY, (x + 1) * NY)

    def spread(row):
        shape = (cell_count, cell_count)
        here = lax.broadcasted_iota(jnp.int32, shape, 0) == lax.broadcasted_iota(jnp.int32, shape, 1)
        column = jnp.sum(jnp.where(here, row, 0.0), axis=1, keepdims=True)
        return jnp.broadcast_to(column, (cell_count, LANES))

    def summed_layers(row):
        shape = (NY, cell_count)
        cell_y = lax.rem(lax.broadcasted_iota(jnp.int32, shape, 1), NY)
        here = lax.broadcasted_iota(jnp.int32, shape, 0) == cell_y
        column = jnp.sum(jnp.where(here, row, 0.0), axis=1, keepdims=True)
        return jnp.broadcast_to(column, (NY, LANES))

    def lanes(block):
        return pl.ds(pl.multiple_of(block * LANES, LANES), LANES)

    def turn_of(index):
        return lax.rem(pos + 1 + index, half)

    def own_slot(part, who, share):
        return gathered[part].at[pl.ds(who * blocks + share * piece, piece)]

    def gather_copy(part, to, source, send_sem, share):
        return pltpu.make_async_remote_copy(
            src_ref=own_slot(part, source, share),
            dst_ref=own_slot(part, source, share),
            send_sem=send_sem.at[share],
            recv_sem=gather_recv.at[part, source, share],
            device_id={"cell": cell, "lev": to},
            device_id_type=MESH,
        )

    def partner_copy(part, who):
        return pltpu.make_async_remote_copy(
            src_ref=gathered[part].at[pl.ds(who * blocks, blocks)],
            dst_ref=gathered[part].at[pl.ds(who * blocks, blocks)],
            send_sem=partner_send.at[part],
            recv_sem=partner_recv.at[part],
            device_id={"cell": cell, "lev": partner},
            device_id_type=MESH,
        )

    def halo_copy(part):
        return pltpu.make_async_remote_copy(
            src_ref=gathered[part].at[pl.ds(lev * blocks, blocks), pl.ds(cell_count - NY, NY)],
            dst_ref=halo.at[part],
            send_sem=halo_send.at[part],
            recv_sem=halo_recv.at[part],
            device_id={"cell": lax.rem(cell + 1, strips), "lev": lev},
            device_id_type=MESH,
        )

    def column_copy(step):
        to = lax.rem(cell + step, strips)
        return pltpu.make_async_remote_copy(
            src_ref=columns.at[cell],
            dst_ref=columns.at[cell],
            send_sem=column_send.at[step],
            recv_sem=column_recv.at[step],
            device_id={"cell": to, "lev": lev},
            device_id_type=MESH,
        )

    def near_copy(part, share, who):
        return pltpu.make_async_remote_copy(
            src_ref=out_one.at[part, share],
            dst_ref=in_near.at[part, who],
            send_sem=near_send.at[part, share],
            recv_sem=near_recv.at[part, who],
            device_id={"cell": base + share, "lev": lev},
            device_id_type=MESH,
        )

    def far_copy(part, share, who):
        return pltpu.make_async_remote_copy(
            src_ref=out_one.at[part, share, side],
            dst_ref=in_far.at[part, who],
            send_sem=far_send.at[part, share],
            recv_sem=far_recv.at[part, who],
            device_id={"cell": other + share, "lev": lev},
            device_id_type=MESH,
        )

    def two_copy(part, to, who):
        return pltpu.make_async_remote_copy(
            src_ref=out_two.at[part, to],
            dst_ref=in_two.at[part, who],
            send_sem=two_send.at[part, to],
            recv_sem=two_recv.at[part, who],
            device_id={"cell": base + to, "lev": lev},
            device_id_type=MESH,
        )

    def emitted_of(value, block):
        return value * emission_ref[pl.ds(block, 1), :]

    def put(ref, part, index, downs, ups):
        for way, values in enumerate((downs, ups)):
            means = []
            for place, value in enumerate(values):
                mean = jnp.mean(value, axis=0, keepdims=True).astype(jnp.bfloat16).astype(jnp.float32)
                ref[part, index, way, place] = (value - mean).astype(jnp.bfloat16)
                means.append(mean)
            means.append(jnp.zeros((NY - len(means), LANES), jnp.float32))
            ref[part, index, way, piece] = jnp.concatenate(means, axis=0).astype(jnp.bfloat16)

    def got(message, b):
        means = message[piece].astype(jnp.float32)
        return message[b].astype(jnp.float32) + means[b : b + 1]

    def get(ref, part, index, b):
        return tuple(got(ref.at[part, index, way], b) for way in range(2))

    def lower(part, block, value):
        gathered[part][lev * blocks + block] = value.astype(jnp.bfloat16)

    def summarize(part, share, values):
        downs, ups = [], []
        for b in range(piece):
            block = share * piece + b
            through = [passing[block, rows(x), :] for x in range(layers)]
            emit = [emitted_of(values[b][x], block) for x in range(layers)]
            down, up = emit[0], emit[-1]
            for x in range(1, layers):
                down = through[x] * down + emit[x]
                up = through[layers - 1 - x] * up + emit[layers - 1 - x]
            downs.append(down)
            ups.append(up)
        put(out_one, part, share, downs, ups)

    def send_summary(part, share):
        far_copy(part, share, slot).start()

        @pl.when(share != pos)
        def _():
            near_copy(part, share, pos).start()

        @pl.when(share == pos)
        def _():
            in_near[part, pos] = out_one[part, pos]

    def load_start(block):
        return [p_ref[rows(x), lanes(block)] for x in range(layers)]

    def start_gather(part, share):
        for step in range(1, groups // 2):
            to = lax.rem(lev + 2 * step, groups)
            gather_copy(part, to, lev, gather_send.at[part, step], share).start()

    def start_halo(part):
        @pl.when(cell < strips - 1)
        def _():
            halo_copy(part).start()

    def lower_start(block, _):
        lower(0, block, p_ref[:, lanes(block)])
        return 0

    operands[0].wait()
    lax.fori_loop(0, blocks, lower_start, 0, unroll=4)
    operands[1].wait()
    columns[cell] = absorber_ref[...]
    pl.semaphore_wait(barrier, greeted)
    for index in range(half):
        start_gather(0, turn_of(index))
    partner_copy(0, lev).start()
    for step in range(1, strips):
        column_copy(step).start()

    for copy in operands[2:]:
        copy.wait()
    coef[0] = spread(absorber_ref[...])

    def summarize_start(index, _):
        share = turn_of(index)
        values = []
        for b in range(piece):
            block = share * piece + b
            passing[block] = jnp.exp(-(coef[0] * cross_ref[pl.ds(block, 1), :]))
            values.append(load_start(block))
        summarize(0, share, values)
        send_summary(0, share)
        return 0

    lax.fori_loop(0, half, summarize_start, 0)
    start_halo(0)
    coef[1] = spread(stream_ref[...])
    coef[2] = spread(turn_ref[...])
    coef[3] = spread(bracket_ref[...].astype(jnp.float32))

    @pl.when(cell == 0)
    def _():
        for part in range(2):
            for block in range(blocks):
                halo[part, block] = inflow_ref[:, block * LANES : (block + 1) * LANES].astype(
                    jnp.bfloat16
                )

    fetch.wait()

    def turn_tables(row, _):
        for bracket in range(brackets):
            for k in range(nonzero):
                rates[bracket, row, k] = rates[bracket, row, k].T
        return 0

    lax.fori_loop(0, blocks, turn_tables, 0, unroll=2)
    for step in range(1, strips):
        column_copy(step).wait()

    def share_block(index, _):
        near = summed_layers(columns[base + index])
        far = summed_layers(columns[other + index + (1 - side) * (half - 1 - 2 * index)])
        for b in range(piece):
            cross = cross_ref[pl.ds(pos * piece + b, 1), :]
            near_pass[index, b] = jnp.exp(-(near * cross))
            far_pass[index, b] = jnp.exp(-(far * cross))
        return 0

    lax.fori_loop(0, half, share_block, 0)

    def enter(part):
        for index in range(half):
            far_copy(part, index, index).wait_recv()
        for step in range(1, half):
            near_copy(part, pos, lax.rem(pos + step, half)).wait_recv()
        below = [[] for _ in range(half)]
        above = [[] for _ in range(half)]
        for b in range(piece):
            beyond = jnp.zeros((NY, LANES), jnp.float32)
            for index in range(half):
                beyond = far_pass[index, b] * beyond + got(in_far.at[part, index], b)
            parts = [get(in_near, part, index, b) for index in range(half)]
            running = jnp.where(side == 1, beyond, 0.0)
            for index in range(half):
                below[index].append(running)
                running = near_pass[index, b] * running + parts[index][0]
            running = jnp.where(side == 0, beyond, 0.0)
            for index in reversed(range(half)):
                above[index].append(running)
                running = near_pass[index, b] * running + parts[index][1]
        for index in range(half):
            put(out_two, part, index, below[index], above[index])
        for step in range(1, half):
            two_copy(part, lax.rem(pos + step, half), pos).start()
        in_two[part, pos] = out_two[part, pos]

    def forward(part, share):
        for step in range(1, groups // 2):
            source = lax.rem(lev + 2 * step, groups)
            gather_copy(part, lev, source, gather_send.at[part, step], share).wait_recv()
            gather_copy(part, partner, source, forward_send.at[part, step], share).start()

    def all_gathered(part):
        partner_copy(part, partner).wait_recv()
        for index in range(half):
            for step in range(1, groups // 2):
                source = lax.rem(partner + 2 * step, groups)
                gather_copy(part, lev, source, gather_send.at[part, step], turn_of(index)).wait_recv()

    def rate_of(part, row):
        picked = jnp.concatenate(
            [gathered[part][pattern_ref[k, row]] for k in range(nonzero)], axis=1
        )
        table = jnp.concatenate(
            [
                jnp.concatenate([rates[bracket, row, k] for k in range(nonzero)], axis=0)
                for bracket in range(brackets)
            ],
            axis=1,
        )
        product = jnp.dot(picked, table, preferred_element_type=jnp.float32)
        kind = coef[3]
        summed = product[:, :LANES]
        for bracket in range(1, brackets):
            summed = jnp.where(
                kind == float(bracket),
                product[:, bracket * LANES : (bracket + 1) * LANES],
                summed,
            )
        return summed

    def finish_transfers(part):
        partner_copy(part, lev).wait_send()
        for index in range(half):
            for step in range(1, groups // 2):
                gather_copy(part, partner, lev, gather_send.at[part, step], index).wait_send()
                gather_copy(part, partner, lev, forward_send.at[part, step], index).wait_send()
            far_copy(part, index, slot).wait_send()
        for step in range(1, half):
            near_copy(part, lax.rem(pos + step, half), pos).wait_send()
            two_copy(part, lax.rem(pos + step, half), pos).wait_send()

        @pl.when(cell < strips - 1)
        def _():
            halo_copy(part).wait_send()

    def before_close(part):
        @pl.when(cell > 0)
        def _():
            halo_copy(part).wait_recv()

    def tendency(part, share, b, value):
        block = share * piece + b
        through = [passing[block, rows(x), :] for x in range(layers)]
        emit = [emitted_of(value[x], block) for x in range(layers)]
        rate_sum = rate_of(part, block)
        down, up = get(in_two, part, share, b)
        downs, ups = [None] * layers, [None] * layers
        for x in range(layers):
            down = through[x] * down + emit[x]
            downs[x] = down
            back = layers - 1 - x
            up = through[back] * up + emit[back]
            ups[back] = up
        arrived = halo[part, block].astype(jnp.float32)
        entering = jnp.where(cell == 0, inflow_ref[:, lanes(block)], arrived)
        gains, total = [], []
        for x in range(layers):
            gained = downs[x] + ups[x] - 2.0 * emit[x]
            taken = (1.0 - through[x]) * gained
            upstream = entering if x == 0 else value[x - 1]
            before_y = pltpu.roll(value[x], 1, 0)
            after_y = pltpu.roll(value[x], NY - 1, 0)
            cross = coef[2, rows(x), :]
            carried = (
                -coef[1, rows(x), :] * (value[x] - upstream)
                - jnp.maximum(cross, 0.0) * (value[x] - before_y)
                - jnp.minimum(cross, 0.0) * (after_y - value[x])
            )
            gains.append(gained)
            total.append(rate_sum[rows(x)] - emit[x] + taken + carried)
        return gains, total

    def exchange(part):
        early = half // 2
        for index in range(early):
            forward(part, turn_of(index))
        enter(part)
        for index in range(early, half):
            forward(part, turn_of(index))
        all_gathered(part)
        before_close(part)

    def arrived_two(part, share):
        @pl.when(share != pos)
        def _():
            two_copy(part, pos, share).wait_recv()

    exchange(0)

    def close_first(index, _):
        share = turn_of(index)
        arrived_two(0, share)
        values = []
        for b in range(piece):
            block = share * piece + b
            value = load_start(block)
            _, total = tendency(0, share, b, value)
            renewed = [value[x] + time_step * total[x] for x in range(layers)]
            for x in range(layers):
                middle[block, rows(x), :] = renewed[x]
            lower(1, block, jnp.concatenate(renewed, axis=0))
            values.append(renewed)
        start_gather(1, share)
        summarize(1, share, values)
        send_summary(1, share)
        return 0

    lax.fori_loop(0, half, close_first, 0)
    partner_copy(1, lev).start()
    start_halo(1)
    finish_transfers(0)
    exchange(1)
    finish_transfers(1)

    def close_second(index, _):
        share = lax.rem(pos + index, half)
        arrived_two(1, share)
        for b in range(piece):
            block = share * piece + b
            value = [middle[block, rows(x), :] for x in range(layers)]
            gains, total = tendency(1, share, b, value)
            for x in range(layers):
                gained_ref[rows(x), lanes(block)] = gains[x]
                advanced_ref[rows(x), lanes(block)] = value[x] + time_step * total[x]
        return 0

    lax.fori_loop(0, half, close_second, 0)


def fused(
    strips,
    groups,
    populations,
    rate_blocks,
    pattern,
    bracket,
    cross_section,
    emission,
    absorber,
    stream_speed,
    cross_speed,
    inflow,
):
    cell_count, level_count = populations.shape
    blocks = level_count // LANES
    half = strips // 2
    piece = blocks // half
    layers_shape = (blocks, cell_count, LANES)
    message = (2, piece + 1, NY, LANES)
    vmem = pl.BlockSpec(memory_space=pltpu.VMEM)
    dma = pltpu.SemaphoreType.DMA
    operands = [
        pattern.T,
        populations,
        rate_blocks,
        bracket.reshape(1, -1),
        absorber.reshape(1, -1),
        stream_speed.reshape(1, -1),
        cross_speed.reshape(1, -1),
        cross_section.reshape(blocks, LANES),
        emission.reshape(blocks, LANES),
        inflow,
    ]
    held = [pltpu.VMEM(value.shape, value.dtype) for value in operands]
    held[0] = pltpu.SMEM(operands[0].shape, operands[0].dtype)
    del held[2]
    return pl.pallas_call(
        functools.partial(fused_kernel, strips, groups),
        out_shape=[pltpu.VMEM((cell_count, level_count), jnp.float32)] * 2,
        in_specs=[pl.BlockSpec(memory_space=pltpu.HBM)] * len(operands),
        out_specs=[vmem, vmem],
        scratch_shapes=held
        + [
            pltpu.VMEM(rate_blocks.shape, rate_blocks.dtype),
            pltpu.VMEM((4, cell_count, LANES), jnp.float32),
            pltpu.VMEM(layers_shape, jnp.float32),
            pltpu.VMEM(layers_shape, jnp.float32),
            pltpu.VMEM((groups * blocks, cell_count, LANES), jnp.bfloat16),
            pltpu.VMEM((groups * blocks, cell_count, LANES), jnp.bfloat16),
            pltpu.VMEM((2, blocks, NY, LANES), jnp.bfloat16),
            pltpu.VMEM((strips, 1, cell_count), jnp.float32),
            pltpu.VMEM((half, piece, NY, LANES), jnp.float32),
            pltpu.VMEM((half, piece, NY, LANES), jnp.float32),
            pltpu.VMEM((2, half) + message, jnp.bfloat16),
            pltpu.VMEM((2, half) + message, jnp.bfloat16),
            pltpu.VMEM((2, half) + message[1:], jnp.bfloat16),
            pltpu.VMEM((2, half) + message, jnp.bfloat16),
            pltpu.VMEM((2, half) + message, jnp.bfloat16),
            dma(()),
            dma((len(held),)),
            dma((2, groups, half)),
            dma((2, groups, half)),
            dma((2, groups, half)),
            dma((2,)),
            dma((2,)),
            dma((2,)),
            dma((2,)),
            dma((strips,)),
            dma((strips,)),
            dma((2, half)),
            dma((2, half)),
            dma((2, half)),
            dma((2, half)),
            dma((2, half)),
            dma((2, half)),
        ],
        compiler_params=pltpu.CompilerParams(
            collective_id=0, has_side_effects=True, vmem_limit_bytes=24 * 1024 * 1024
        ),
    )(*[pltpu.with_memory_space_constraint(value, pltpu.HBM) for value in operands])


def shortened(value):

    def short(part):
        return part.astype(jnp.bfloat16) if part.dtype == jnp.float32 else part

    return jax.tree.map(short, value)


def shifted(value, axis, by):
    peers = lax.axis_size(axis)
    pairs = [(i, i + by) for i in range(peers) if 0 <= i + by < peers]
    return lax.ppermute(value, axis, pairs)


def affine(earlier, later):
    return (earlier[0] * later[0], later[0] * earlier[1] + later[1])


def rate_term(populations, rate_blocks, pattern, bracket):
    lowered = populations.astype(jnp.bfloat16)
    gathered = lax.all_gather(lowered, "lev", axis=1, tiled=True)
    cell_count = gathered.shape[0]
    brackets, rows, nonzero, block_size = rate_blocks.shape[:4]
    by_block = jnp.swapaxes(gathered.reshape(cell_count, -1, block_size), 0, 1)

    def one_row(row):
        summed = jnp.zeros((cell_count, block_size), jnp.float32)
        for bracket_id in range(brackets):
            product = jnp.zeros((cell_count, block_size), jnp.float32)
            for k in range(nonzero):
                column = lax.dynamic_index_in_dim(by_block, pattern[row, k], 0, keepdims=False)
                table = lax.dynamic_index_in_dim(rate_blocks[bracket_id], row, 0, keepdims=False)[k]
                product += jnp.einsum("cj,ij->ci", column, table, preferred_element_type=jnp.float32)
            summed = jnp.where((bracket == bracket_id)[:, None], product, summed)
        return summed

    stacked = lax.map(one_row, jnp.arange(rows, dtype=jnp.int32))
    return jnp.transpose(stacked, (1, 0, 2)).reshape(cell_count, -1)


def entering(received):
    start = jnp.zeros(received.shape[2:], jnp.float32)

    def advance(running, layer_in):
        return (layer_in[0] * running + layer_in[1], running)

    _, from_below = lax.scan(advance, start, (received[:, 0], received[:, 1]))
    _, from_above = lax.scan(advance, start, (received[:, 2], received[:, 3]), reverse=True)
    both_sides = jnp.stack([from_below, from_above], axis=1)
    return lax.all_to_all(both_sides, "cell", split_axis=0, concat_axis=3, tiled=True)


def radiation(populations, emission, cross_section, absorber):
    cell_count, level_count = populations.shape
    strips = cell_count // NY
    emitted = populations * emission[None, :]
    transmit = jnp.exp(-(absorber[:, None] * cross_section[None, :]))
    layered_pass = transmit.reshape(strips, NY, level_count)
    layered_emit = emitted.reshape(strips, NY, level_count)
    passed_down, local_down = lax.associative_scan(affine, (layered_pass, layered_emit), axis=0)
    passed_up, local_up = lax.associative_scan(
        affine, (layered_pass, layered_emit), reverse=True, axis=0
    )
    summary = jnp.stack([passed_down[-1], local_down[-1], passed_up[0], local_up[0]])[None]
    returned = entering(lax.all_to_all(summary, "cell", split_axis=3, concat_axis=0, tiled=True))
    enter_down = returned[0, 0]
    enter_up = returned[0, 1]
    downward = local_down + passed_down * enter_down[None]
    upward = local_up + passed_up * enter_up[None]
    absorbed = (1.0 - layered_pass) * (downward + upward - 2.0 * layered_emit)
    return (emitted, absorbed.reshape(cell_count, level_count))


def advection(populations, inflow, stream_speed, cross_speed):
    cell_count, level_count = populations.shape
    layered = populations.reshape(cell_count // NY, NY, level_count)
    arrived = shifted(shortened(layered[-1]), "cell", 1)
    boundary = jnp.where(lax.axis_index("cell") == 0, inflow, arrived)
    upstream = jnp.concatenate([boundary[None], layered[:-1]], axis=0)
    before_y = jnp.roll(layered, 1, axis=1)
    after_y = jnp.roll(layered, -1, axis=1)
    along_x = stream_speed.reshape(-1, NY, 1)
    along_y = cross_speed.reshape(-1, NY, 1)
    flux_sum = (
        -along_x * (layered - upstream)
        - jnp.maximum(along_y, 0.0) * (layered - before_y)
        - jnp.minimum(along_y, 0.0) * (after_y - layered)
    )
    return flux_sum.reshape(cell_count, level_count)


def tendency(
    populations,
    rate_blocks,
    pattern,
    bracket,
    cross_section,
    emission,
    absorber,
    stream_speed,
    cross_speed,
    inflow,
):
    rates_part = rate_term(populations, rate_blocks, pattern, bracket)
    emitted, absorbed = radiation(populations, emission, cross_section, absorber)
    carried = advection(populations, inflow, stream_speed, cross_speed)
    return (rates_part - emitted + absorbed + carried, absorbed)


def local(
    populations,
    rate_blocks,
    pattern,
    bracket,
    cross_section,
    emission,
    absorber,
    stream_speed,
    cross_speed,
    inflow,
):
    strips, groups = lax.axis_size("cell"), lax.axis_size("lev")
    cell_count, level_count = populations.shape
    if (
        groups % 2 == 0
        and strips % 2 == 0
        and cell_count % NY == 0
        and level_count % (strips // 2 * LANES) == 0
        and rate_blocks.shape[3] == LANES
        and 2 * level_count < strips * LANES * NY
    ):
        advanced, gained = (
            fused(
                strips,
                groups,
                populations,
                rate_blocks,
                pattern,
                bracket,
                cross_section,
                emission,
                absorber,
                stream_speed,
                cross_speed,
                inflow,
            )
        )
        transmit = jnp.exp(-(absorber[:, None] * cross_section[None, :]))
        return (0.5 * (populations + advanced), (1.0 - transmit) * gained)
    first_rate, _ = tendency(
        populations,
        rate_blocks,
        pattern,
        bracket,
        cross_section,
        emission,
        absorber,
        stream_speed,
        cross_speed,
        inflow,
    )
    middle = populations + time_step * first_rate
    second, absorption = tendency(
        middle,
        rate_blocks,
        pattern,
        bracket,
        cross_section,
        emission,
        absorber,
        stream_speed,
        cross_speed,
        inflow,
    )
    updated = 0.5 * (populations + middle + time_step * second)
    return (updated, absorption)


def solution(mesh):
    in_specs = (
        P("cell", "lev"),
        P(None, "lev", None, None, None),
        P("lev", None),
        P("cell"),
        P("lev"),
        P("lev"),
        P("cell"),
        P("cell"),
        P("cell"),
        P(None, "lev"),
    )
    out_specs = (P("cell", "lev"), P("cell", "lev"))
    return jax.shard_map(local, mesh=mesh, in_specs=in_specs, out_specs=out_specs, check_vma=False)
```

```python
import functools

import jax
import jax.numpy as jnp
from jax import lax
from jax.experimental import pallas as pl
from jax.experimental.pallas import tpu as pltpu
from jax.sharding import PartitionSpec as P

NY = 16
LANES = 128

time_step = 0.25

MESH = pl.DeviceIdType.MESH


def fused_kernel(
    strips,
    groups,
    pattern_hbm,
    p_hbm,
    rates_hbm,
    bracket_hbm,
    absorber_hbm,
    stream_hbm,
    turn_hbm,
    cross_hbm,
    emission_hbm,
    inflow_hbm,
    advanced_ref,
    gained_ref,
    pattern_ref,
    p_ref,
    bracket_ref,
    absorber_ref,
    stream_ref,
    turn_ref,
    cross_ref,
    emission_ref,
    inflow_ref,
    rates,
    coef,
    passing,
    middle,
    gathered_first,
    gathered_second,
    halo,
    columns,
    near_pass,
    far_pass,
    out_one,
    in_near,
    in_far,
    out_two,
    in_two,
    rates_sem,
    operand_sem,
    gather_send,
    gather_recv,
    forward_send,
    partner_send,
    partner_recv,
    halo_send,
    halo_recv,
    column_send,
    column_recv,
    near_send,
    near_recv,
    far_send,
    far_recv,
    two_send,
    two_recv,
):
    cell = lax.axis_index("cell")
    lev = lax.axis_index("lev")
    gathered = (gathered_first, gathered_second)
    cell_count = p_ref.shape[0]
    layers = cell_count // NY
    blocks = p_ref.shape[1] // LANES
    half = strips // 2
    piece = blocks // half
    brackets, _, nonzero = rates_hbm.shape[:3]
    partner = lev + 1 - 2 * lax.rem(lev, 2)
    side = cell // half
    pos = lax.rem(cell, half)
    base = side * half
    other = (1 - side) * half
    slot = pos + side * (half - 1 - 2 * pos)

    barrier = pltpu.get_barrier_semaphore()
    greeted = 0
    for step in range(1, strips):
        pl.semaphore_signal(
            barrier,
            inc=1,
            device_id={"cell": lax.rem(cell + step, strips), "lev": lev},
            device_id_type=MESH,
        )
        greeted += 1
    for step in range(1, groups // 2):
        pl.semaphore_signal(
            barrier,
            inc=1,
            device_id={"cell": cell, "lev": lax.rem(lev + 2 * step, groups)},
            device_id_type=MESH,
        )
        greeted += 1
    pl.semaphore_signal(barrier, inc=1, device_id={"cell": cell, "lev": partner}, device_id_type=MESH)
    greeted += 1

    operands = [
        pltpu.make_async_copy(source, into, operand_sem.at[index])
        for index, (source, into) in enumerate(
            (
                (p_hbm, p_ref),
                (absorber_hbm, absorber_ref),
                (cross_hbm, cross_ref),
                (emission_hbm, emission_ref),
                (stream_hbm, stream_ref),
                (turn_hbm, turn_ref),
                (bracket_hbm, bracket_ref),
                (inflow_hbm, inflow_ref),
                (pattern_hbm, pattern_ref),
            )
        )
    ]
    for copy in operands:
        copy.start()
    fetch = pltpu.make_async_copy(rates_hbm, rates, rates_sem)
    fetch.start()

    def rows(x):
        return slice(x * NY, (x + 1) * NY)

    def spread(row):
        shape = (cell_count, cell_count)
        here = lax.broadcasted_iota(jnp.int32, shape, 0) == lax.broadcasted_iota(jnp.int32, shape, 1)
        column = jnp.sum(jnp.where(here, row, 0.0), axis=1, keepdims=True)
        return jnp.broadcast_to(column, (cell_count, LANES))

    def summed_layers(row):
        shape = (NY, cell_count)
        cell_y = lax.rem(lax.broadcasted_iota(jnp.int32, shape, 1), NY)
        here = lax.broadcasted_iota(jnp.int32, shape, 0) == cell_y
        column = jnp.sum(jnp.where(here, row, 0.0), axis=1, keepdims=True)
        return jnp.broadcast_to(column, (NY, LANES))

    def lanes(block):
        return pl.ds(pl.multiple_of(block * LANES, LANES), LANES)

    def turn_of(index):
        return lax.rem(pos + 1 + index, half)

    def own_slot(part, who, share):
        return gathered[part].at[pl.ds(who * blocks + share * piece, piece)]

    def gather_copy(part, to, source, send_sem, share):
        return pltpu.make_async_remote_copy(
            src_ref=own_slot(part, source, share),
            dst_ref=own_slot(part, source, share),
            send_sem=send_sem.at[share],
            recv_sem=gather_recv.at[part, source, share],
            device_id={"cell": cell, "lev": to},
            device_id_type=MESH,
        )

    def partner_copy(part, who):
        return pltpu.make_async_remote_copy(
            src_ref=gathered[part].at[pl.ds(who * blocks, blocks)],
            dst_ref=gathered[part].at[pl.ds(who * blocks, blocks)],
            send_sem=partner_send.at[part],
            recv_sem=partner_recv.at[part],
            device_id={"cell": cell, "lev": partner},
            device_id_type=MESH,
        )

    def halo_copy(part):
        return pltpu.make_async_remote_copy(
            src_ref=gathered[part].at[pl.ds(lev * blocks, blocks), pl.ds(cell_count - NY, NY)],
            dst_ref=halo.at[part],
            send_sem=halo_send.at[part],
            recv_sem=halo_recv.at[part],
            device_id={"cell": lax.rem(cell + 1, strips), "lev": lev},
            device_id_type=MESH,
        )

    def column_copy(step):
        to = lax.rem(cell + step, strips)
        return pltpu.make_async_remote_copy(
            src_ref=columns.at[cell],
            dst_ref=columns.at[cell],
            send_sem=column_send.at[step],
            recv_sem=column_recv.at[step],
            device_id={"cell": to, "lev": lev},
            device_id_type=MESH,
        )

    def near_copy(part, share, who):
        return pltpu.make_async_remote_copy(
            src_ref=out_one.at[part, share],
            dst_ref=in_near.at[part, who],
            send_sem=near_send.at[part, share],
            recv_sem=near_recv.at[part, who],
            device_id={"cell": base + share, "lev": lev},
            device_id_type=MESH,
        )

    def far_copy(part, share, who):
        return pltpu.make_async_remote_copy(
            src_ref=out_one.at[part, share, pl.ds(piece * side, piece)],
            dst_ref=in_far.at[part, who],
            send_sem=far_send.at[part, share],
            recv_sem=far_recv.at[part, who],
            device_id={"cell": other + share, "lev": lev},
            device_id_type=MESH,
        )

    def two_copy(part, to, who):
        return pltpu.make_async_remote_copy(
            src_ref=out_two.at[part, to],
            dst_ref=in_two.at[part, who],
            send_sem=two_send.at[part, to],
            recv_sem=two_recv.at[part, who],
            device_id={"cell": base + to, "lev": lev},
            device_id_type=MESH,
        )

    def emitted_of(value, block):
        return value * emission_ref[pl.ds(block, 1), :]

    def put(ref, part, index, downs, ups):
        means = []
        for place, value in enumerate(downs + ups):
            mean = jnp.mean(value, axis=0, keepdims=True).astype(jnp.bfloat16).astype(jnp.float32)
            ref[part, index, place + place // piece] = (value - mean).astype(jnp.bfloat16)
            means.append(mean)
        if len(means) < NY:
            means.append(jnp.zeros((NY - len(means), LANES), jnp.float32))
        ref[part, index, piece] = jnp.concatenate(means, axis=0).astype(jnp.bfloat16)

    def get(ref, part, index, b):
        means = ref[part, index, piece].astype(jnp.float32)
        return tuple(
            ref[part, index, place + place // piece].astype(jnp.float32) + means[place : place + 1]
            for place in (b, piece + b)
        )

    def is_first():
        return lax.broadcasted_iota(jnp.int32, (NY, LANES), 0) == 0

    def put_sums(part, share, downs, ups):
        for place, value in enumerate(downs + ups):
            first = value[:1].astype(jnp.bfloat16).astype(jnp.float32)
            out_one[part, share, place] = jnp.where(is_first(), value, value - first).astype(
                jnp.bfloat16
            )

    def restored(tile):
        value = tile.astype(jnp.float32)
        return jnp.where(is_first(), value, value + value[:1])

    def lower(part, block, value):
        gathered[part][lev * blocks + block] = value.astype(jnp.bfloat16)

    def summarize(part, share, values):
        downs, ups = [], []
        for b in range(piece):
            block = share * piece + b
            through = [passing[block, rows(x), :] for x in range(layers)]
            emit = [emitted_of(values[b][x], block) for x in range(layers)]
            down, up = emit[0], emit[-1]
            for x in range(1, layers):
                down = through[x] * down + emit[x]
                up = through[layers - 1 - x] * up + emit[layers - 1 - x]
            downs.append(down)
            ups.append(up)
        put_sums(part, share, downs, ups)

    def send_summary(part, share):
        far_copy(part, share, slot).start()

        @pl.when(share != pos)
        def _():
            near_copy(part, share, pos).start()

        @pl.when(share == pos)
        def _():
            in_near[part, pos] = out_one[part, pos]

    def load_start(block):
        return [p_ref[rows(x), lanes(block)] for x in range(layers)]

    def start_gather(part, share):
        for step in range(1, groups // 2):
            to = lax.rem(lev + 2 * step, groups)
            gather_copy(part, to, lev, gather_send.at[part, step], share).start()

    def start_halo(part):
        @pl.when(cell < strips - 1)
        def _():
            halo_copy(part).start()

    def lower_start(block, _):
        lower(0, block, p_ref[:, lanes(block)])
        return 0

    def summarize_start(index, _):
        share = turn_of(index)
        values = []
        for b in range(piece):
            block = share * piece + b
            passing[block] = jnp.exp(-(coef[0] * cross_ref[pl.ds(block, 1), :]))
            values.append(load_start(block))
        summarize(0, share, values)
        return 0

    for copy in operands[:4]:
        copy.wait()
    lax.fori_loop(0, blocks, lower_start, 0, unroll=4)
    columns[cell] = absorber_ref[...]
    coef[0] = spread(absorber_ref[...])
    lax.fori_loop(0, half, summarize_start, 0)
    pl.semaphore_wait(barrier, greeted)
    for step in range(1, strips):
        column_copy(step).start()
    start_gather(0, turn_of(0))
    for index in range(half):
        send_summary(0, turn_of(index))
    start_gather(0, turn_of(1))
    for index in range(2, half):
        start_gather(0, turn_of(index))
    partner_copy(0, lev).start()
    for copy in operands[4:]:
        copy.wait()
    start_halo(0)
    coef[1] = spread(stream_ref[...])
    coef[2] = spread(turn_ref[...])
    coef[3] = spread(bracket_ref[...].astype(jnp.float32))

    @pl.when(cell == 0)
    def _():
        for part in range(2):
            for block in range(blocks):
                halo[part, block] = inflow_ref[:, block * LANES : (block + 1) * LANES].astype(
                    jnp.bfloat16
                )

    fetch.wait()

    def turn_tables(row, _):
        for bracket in range(brackets):
            for k in range(nonzero):
                rates[bracket, row, k] = rates[bracket, row, k].T
        return 0

    lax.fori_loop(0, blocks, turn_tables, 0, unroll=2)
    for step in range(1, strips):
        column_copy(step).wait()

    def share_block(index, _):
        near = summed_layers(columns[base + index])
        far = summed_layers(columns[other + index + (1 - side) * (half - 1 - 2 * index)])
        for b in range(piece):
            cross = cross_ref[pl.ds(pos * piece + b, 1), :]
            near_pass[index, b] = jnp.exp(-(near * cross))
            far_pass[index, b] = jnp.exp(-(far * cross))
        return 0

    lax.fori_loop(0, half, share_block, 0)

    def enter(part):
        for index in range(half):
            far_copy(part, index, index).wait_recv()
        for step in range(1, half):
            near_copy(part, pos, lax.rem(pos + step, half)).wait_recv()
        below = [[] for _ in range(half)]
        above = [[] for _ in range(half)]
        for b in range(piece):
            beyond = jnp.zeros((NY, LANES), jnp.float32)
            for index in range(half):
                beyond = far_pass[index, b] * beyond + restored(in_far[part, index, b])
            parts = [
                (restored(in_near[part, index, b]), restored(in_near[part, index, piece + b]))
                for index in range(half)
            ]
            running = jnp.where(side == 1, beyond, 0.0)
            for index in range(half):
                below[index].append(running)
                running = near_pass[index, b] * running + parts[index][0]
            running = jnp.where(side == 0, beyond, 0.0)
            for index in reversed(range(half)):
                above[index].append(running)
                running = near_pass[index, b] * running + parts[index][1]
        for index in range(half):
            put(out_two, part, index, below[index], above[index])
        for step in range(1, half):
            two_copy(part, lax.rem(pos + step, half), pos).start()
        in_two[part, pos] = out_two[part, pos]

    def forward(part, share):
        for step in range(1, groups // 2):
            source = lax.rem(lev + 2 * step, groups)
            gather_copy(part, lev, source, gather_send.at[part, step], share).wait_recv()
            gather_copy(part, partner, source, forward_send.at[part, step], share).start()

    def all_gathered(part):
        partner_copy(part, partner).wait_recv()
        for index in range(half):
            for step in range(1, groups // 2):
                source = lax.rem(partner + 2 * step, groups)
                gather_copy(part, lev, source, gather_send.at[part, step], turn_of(index)).wait_recv()

    def rate_row(part, row):
        picked = jnp.concatenate(
            [gathered[part][pattern_ref[k, row]] for k in range(nonzero)], axis=1
        )
        table = jnp.concatenate(
            [
                jnp.concatenate([rates[bracket, row, k] for k in range(nonzero)], axis=0)
                for bracket in range(brackets)
            ],
            axis=1,
        )
        product = jnp.dot(picked, table, preferred_element_type=jnp.float32)
        kind = coef[3]
        summed = product[:, :LANES]
        for bracket in range(1, brackets):
            summed = jnp.where(
                kind == float(bracket),
                product[:, bracket * LANES : (bracket + 1) * LANES],
                summed,
            )
        return summed

    def finish_transfers(part):
        partner_copy(part, lev).wait_send()
        for index in range(half):
            for step in range(1, groups // 2):
                gather_copy(part, partner, lev, gather_send.at[part, step], index).wait_send()
                gather_copy(part, partner, lev, forward_send.at[part, step], index).wait_send()
            far_copy(part, index, slot).wait_send()
        for step in range(1, half):
            near_copy(part, lax.rem(pos + step, half), pos).wait_send()
            two_copy(part, lax.rem(pos + step, half), pos).wait_send()

        @pl.when(cell < strips - 1)
        def _():
            halo_copy(part).wait_send()

    def before_close(part):
        @pl.when(cell > 0)
        def _():
            halo_copy(part).wait_recv()

    def rates_of(part, share):
        return [rate_row(part, share * piece + b) for b in range(piece)]

    def tendency(part, share, b, value, rate_sum):
        block = share * piece + b
        through = [passing[block, rows(x), :] for x in range(layers)]
        emit = [emitted_of(value[x], block) for x in range(layers)]
        down, up = get(in_two, part, share, b)
        downs, ups = [None] * layers, [None] * layers
        for x in range(layers):
            down = through[x] * down + emit[x]
            downs[x] = down
            back = layers - 1 - x
            up = through[back] * up + emit[back]
            ups[back] = up
        arrived = halo[part, block].astype(jnp.float32)
        entering = jnp.where(cell == 0, inflow_ref[:, lanes(block)], arrived)
        gains, total = [], []
        for x in range(layers):
            gained = downs[x] + ups[x] - 2.0 * emit[x]
            taken = (1.0 - through[x]) * gained
            upstream = entering if x == 0 else value[x - 1]
            before_y = pltpu.roll(value[x], 1, 0)
            after_y = pltpu.roll(value[x], NY - 1, 0)
            cross = coef[2, rows(x), :]
            carried = (
                -coef[1, rows(x), :] * (value[x] - upstream)
                - jnp.maximum(cross, 0.0) * (value[x] - before_y)
                - jnp.minimum(cross, 0.0) * (after_y - value[x])
            )
            gains.append(gained)
            total.append(rate_sum[rows(x)] - emit[x] + taken + carried)
        return gains, total

    def exchange(part):
        early = half // 2
        for index in range(early):
            forward(part, turn_of(index))
        enter(part)
        for index in range(early, half):
            forward(part, turn_of(index))
        all_gathered(part)
        before_close(part)

    def arrived_two(part, share):
        @pl.when(share != pos)
        def _():
            two_copy(part, pos, share).wait_recv()

    exchange(0)

    def close_first(share, sums):
        arrived_two(0, share)
        values = []
        for b in range(piece):
            block = share * piece + b
            value = load_start(block)
            _, total = tendency(0, share, b, value, sums[b])
            renewed = [value[x] + time_step * total[x] for x in range(layers)]
            for x in range(layers):
                middle[block, rows(x), :] = renewed[x]
            lower(1, block, jnp.concatenate(renewed, axis=0))
            values.append(renewed)
        start_gather(1, share)
        summarize(1, share, values)
        send_summary(1, share)

    ready = [rates_of(0, turn_of(index)) for index in range(min(2, half))]
    for index in range(half):
        if index + 2 < half:
            ready.append(rates_of(0, turn_of(index + 2)))
        close_first(turn_of(index), ready[index])
    partner_copy(1, lev).start()
    start_halo(1)
    finish_transfers(0)
    exchange(1)
    finish_transfers(1)

    def close_second(share, sums):
        arrived_two(1, share)
        for b in range(piece):
            block = share * piece + b
            value = [middle[block, rows(x), :] for x in range(layers)]
            gains, total = tendency(1, share, b, value, sums[b])
            for x in range(layers):
                gained_ref[rows(x), lanes(block)] = gains[x]
                advanced_ref[rows(x), lanes(block)] = value[x] + time_step * total[x]

    def own_first(index):
        return lax.rem(pos + index, half)

    ready = [rates_of(1, own_first(index)) for index in range(min(2, half))]
    for index in range(half):
        if index + 2 < half:
            ready.append(rates_of(1, own_first(index + 2)))
        close_second(own_first(index), ready[index])


def fused(
    strips,
    groups,
    populations,
    rate_blocks,
    pattern,
    bracket,
    cross_section,
    emission,
    absorber,
    stream_speed,
    cross_speed,
    inflow,
):
    cell_count, level_count = populations.shape
    blocks = level_count // LANES
    half = strips // 2
    piece = blocks // half
    layers_shape = (blocks, cell_count, LANES)
    message = (2 * piece + 1, NY, LANES)
    vmem = pl.BlockSpec(memory_space=pltpu.VMEM)
    dma = pltpu.SemaphoreType.DMA
    operands = [
        pattern.T,
        populations,
        rate_blocks,
        bracket.reshape(1, -1),
        absorber.reshape(1, -1),
        stream_speed.reshape(1, -1),
        cross_speed.reshape(1, -1),
        cross_section.reshape(blocks, LANES),
        emission.reshape(blocks, LANES),
        inflow,
    ]
    held = [pltpu.VMEM(value.shape, value.dtype) for value in operands]
    held[0] = pltpu.SMEM(operands[0].shape, operands[0].dtype)
    del held[2]
    return pl.pallas_call(
        functools.partial(fused_kernel, strips, groups),
        out_shape=[pltpu.VMEM((cell_count, level_count), jnp.float32)] * 2,
        in_specs=[pl.BlockSpec(memory_space=pltpu.HBM)] * len(operands),
        out_specs=[vmem, vmem],
        scratch_shapes=held
        + [
            pltpu.VMEM(rate_blocks.shape, rate_blocks.dtype),
            pltpu.VMEM((4, cell_count, LANES), jnp.float32),
            pltpu.VMEM(layers_shape, jnp.float32),
            pltpu.VMEM(layers_shape, jnp.float32),
            pltpu.VMEM((groups * blocks, cell_count, LANES), jnp.bfloat16),
            pltpu.VMEM((groups * blocks, cell_count, LANES), jnp.bfloat16),
            pltpu.VMEM((2, blocks, NY, LANES), jnp.bfloat16),
            pltpu.VMEM((strips, 1, cell_count), jnp.float32),
            pltpu.VMEM((half, piece, NY, LANES), jnp.float32),
            pltpu.VMEM((half, piece, NY, LANES), jnp.float32),
            pltpu.VMEM((2, half, 2 * piece, NY, LANES), jnp.bfloat16),
            pltpu.VMEM((2, half, 2 * piece, NY, LANES), jnp.bfloat16),
            pltpu.VMEM((2, half, piece, NY, LANES), jnp.bfloat16),
            pltpu.VMEM((2, half) + message, jnp.bfloat16),
            pltpu.VMEM((2, half) + message, jnp.bfloat16),
            dma(()),
            dma((len(held),)),
            dma((2, groups, half)),
            dma((2, groups, half)),
            dma((2, groups, half)),
            dma((2,)),
            dma((2,)),
            dma((2,)),
            dma((2,)),
            dma((strips,)),
            dma((strips,)),
            dma((2, half)),
            dma((2, half)),
            dma((2, half)),
            dma((2, half)),
            dma((2, half)),
            dma((2, half)),
        ],
        compiler_params=pltpu.CompilerParams(
            collective_id=0, has_side_effects=True, vmem_limit_bytes=24 * 1024 * 1024
        ),
    )(*[pltpu.with_memory_space_constraint(value, pltpu.HBM) for value in operands])


def shortened(value):

    def short(part):
        return part.astype(jnp.bfloat16) if part.dtype == jnp.float32 else part

    return jax.tree.map(short, value)


def shifted(value, axis, by):
    peers = lax.axis_size(axis)
    pairs = [(i, i + by) for i in range(peers) if 0 <= i + by < peers]
    return lax.ppermute(value, axis, pairs)


def affine(earlier, later):
    return (earlier[0] * later[0], later[0] * earlier[1] + later[1])


def rate_term(populations, rate_blocks, pattern, bracket):
    lowered = populations.astype(jnp.bfloat16)
    gathered = lax.all_gather(lowered, "lev", axis=1, tiled=True)
    cell_count = gathered.shape[0]
    brackets, rows, nonzero, block_size = rate_blocks.shape[:4]
    by_block = jnp.swapaxes(gathered.reshape(cell_count, -1, block_size), 0, 1)

    def one_row(row):
        summed = jnp.zeros((cell_count, block_size), jnp.float32)
        for bracket_id in range(brackets):
            product = jnp.zeros((cell_count, block_size), jnp.float32)
            for k in range(nonzero):
                column = lax.dynamic_index_in_dim(by_block, pattern[row, k], 0, keepdims=False)
                table = lax.dynamic_index_in_dim(rate_blocks[bracket_id], row, 0, keepdims=False)[k]
                product += jnp.einsum("cj,ij->ci", column, table, preferred_element_type=jnp.float32)
            summed = jnp.where((bracket == bracket_id)[:, None], product, summed)
        return summed

    stacked = lax.map(one_row, jnp.arange(rows, dtype=jnp.int32))
    return jnp.transpose(stacked, (1, 0, 2)).reshape(cell_count, -1)


def entering(received):
    start = jnp.zeros(received.shape[2:], jnp.float32)

    def advance(running, layer_in):
        return (layer_in[0] * running + layer_in[1], running)

    _, from_below = lax.scan(advance, start, (received[:, 0], received[:, 1]))
    _, from_above = lax.scan(advance, start, (received[:, 2], received[:, 3]), reverse=True)
    both_sides = jnp.stack([from_below, from_above], axis=1)
    return lax.all_to_all(both_sides, "cell", split_axis=0, concat_axis=3, tiled=True)


def radiation(populations, emission, cross_section, absorber):
    cell_count, level_count = populations.shape
    strips = cell_count // NY
    emitted = populations * emission[None, :]
    transmit = jnp.exp(-(absorber[:, None] * cross_section[None, :]))
    layered_pass = transmit.reshape(strips, NY, level_count)
    layered_emit = emitted.reshape(strips, NY, level_count)
    passed_down, local_down = lax.associative_scan(affine, (layered_pass, layered_emit), axis=0)
    passed_up, local_up = lax.associative_scan(
        affine, (layered_pass, layered_emit), reverse=True, axis=0
    )
    summary = jnp.stack([passed_down[-1], local_down[-1], passed_up[0], local_up[0]])[None]
    returned = entering(lax.all_to_all(summary, "cell", split_axis=3, concat_axis=0, tiled=True))
    enter_down = returned[0, 0]
    enter_up = returned[0, 1]
    downward = local_down + passed_down * enter_down[None]
    upward = local_up + passed_up * enter_up[None]
    absorbed = (1.0 - layered_pass) * (downward + upward - 2.0 * layered_emit)
    return (emitted, absorbed.reshape(cell_count, level_count))


def advection(populations, inflow, stream_speed, cross_speed):
    cell_count, level_count = populations.shape
    layered = populations.reshape(cell_count // NY, NY, level_count)
    arrived = shifted(shortened(layered[-1]), "cell", 1)
    boundary = jnp.where(lax.axis_index("cell") == 0, inflow, arrived)
    upstream = jnp.concatenate([boundary[None], layered[:-1]], axis=0)
    before_y = jnp.roll(layered, 1, axis=1)
    after_y = jnp.roll(layered, -1, axis=1)
    along_x = stream_speed.reshape(-1, NY, 1)
    along_y = cross_speed.reshape(-1, NY, 1)
    flux_sum = (
        -along_x * (layered - upstream)
        - jnp.maximum(along_y, 0.0) * (layered - before_y)
        - jnp.minimum(along_y, 0.0) * (after_y - layered)
    )
    return flux_sum.reshape(cell_count, level_count)


def tendency(
    populations,
    rate_blocks,
    pattern,
    bracket,
    cross_section,
    emission,
    absorber,
    stream_speed,
    cross_speed,
    inflow,
):
    rates_part = rate_term(populations, rate_blocks, pattern, bracket)
    emitted, absorbed = radiation(populations, emission, cross_section, absorber)
    carried = advection(populations, inflow, stream_speed, cross_speed)
    return (rates_part - emitted + absorbed + carried, absorbed)


def local(
    populations,
    rate_blocks,
    pattern,
    bracket,
    cross_section,
    emission,
    absorber,
    stream_speed,
    cross_speed,
    inflow,
):
    strips, groups = lax.axis_size("cell"), lax.axis_size("lev")
    cell_count, level_count = populations.shape
    if (
        groups % 2 == 0
        and strips % 2 == 0
        and cell_count % NY == 0
        and level_count % (strips // 2 * LANES) == 0
        and rate_blocks.shape[3] == LANES
        and 4 * level_count <= strips * LANES * NY
    ):
        advanced, gained = (
            fused(
                strips,
                groups,
                populations,
                rate_blocks,
                pattern,
                bracket,
                cross_section,
                emission,
                absorber,
                stream_speed,
                cross_speed,
                inflow,
            )
        )
        transmit = jnp.exp(-(absorber[:, None] * cross_section[None, :]))
        return (0.5 * (populations + advanced), (1.0 - transmit) * gained)
    first_rate, _ = tendency(
        populations,
        rate_blocks,
        pattern,
        bracket,
        cross_section,
        emission,
        absorber,
        stream_speed,
        cross_speed,
        inflow,
    )
    middle = populations + time_step * first_rate
    second, absorption = tendency(
        middle,
        rate_blocks,
        pattern,
        bracket,
        cross_section,
        emission,
        absorber,
        stream_speed,
        cross_speed,
        inflow,
    )
    updated = 0.5 * (populations + middle + time_step * second)
    return (updated, absorption)


def solution(mesh):
    in_specs = (
        P("cell", "lev"),
        P(None, "lev", None, None, None),
        P("lev", None),
        P("cell"),
        P("lev"),
        P("lev"),
        P("cell"),
        P("cell"),
        P("cell"),
        P(None, "lev"),
    )
    out_specs = (P("cell", "lev"), P("cell", "lev"))
    return jax.shard_map(local, mesh=mesh, in_specs=in_specs, out_specs=out_specs, check_vma=False)
```

```python
import functools

import jax
import jax.numpy as jnp
from jax import lax
from jax.experimental import pallas as pl
from jax.experimental.pallas import tpu as pltpu
from jax.sharding import PartitionSpec as P

NY = 16
LANES = 128

time_step = 0.25

MESH = pl.DeviceIdType.MESH


def fused_kernel(
    strips,
    groups,
    pattern_hbm,
    p_hbm,
    rates_hbm,
    bracket_hbm,
    absorber_hbm,
    stream_hbm,
    turn_hbm,
    cross_hbm,
    emission_hbm,
    inflow_hbm,
    advanced_ref,
    gained_ref,
    pattern_ref,
    p_ref,
    bracket_ref,
    absorber_ref,
    stream_ref,
    turn_ref,
    cross_ref,
    emission_ref,
    inflow_ref,
    rates,
    coef,
    passing,
    middle,
    known,
    inside,
    from_below,
    from_above,
    gathered_first,
    gathered_second,
    halo,
    columns,
    near_pass,
    far_pass,
    out_one,
    in_near,
    in_far,
    out_two,
    in_two,
    rates_sem,
    operand_sem,
    gather_send,
    gather_recv,
    forward_send,
    partner_send,
    partner_recv,
    halo_send,
    halo_recv,
    column_send,
    column_recv,
    near_send,
    near_recv,
    far_send,
    far_recv,
    two_send,
    two_recv,
):
    cell = lax.axis_index("cell")
    lev = lax.axis_index("lev")
    gathered = (gathered_first, gathered_second)
    cell_count = p_ref.shape[0]
    layers = cell_count // NY
    blocks = p_ref.shape[1] // LANES
    half = strips // 2
    piece = blocks // half
    brackets, _, nonzero = rates_hbm.shape[:3]
    partner = lev + 1 - 2 * lax.rem(lev, 2)
    side = cell // half
    pos = lax.rem(cell, half)
    base = side * half
    other = (1 - side) * half
    slot = pos + side * (half - 1 - 2 * pos)

    barrier = pltpu.get_barrier_semaphore()
    greeted = 0
    for step in range(1, strips):
        pl.semaphore_signal(
            barrier,
            inc=1,
            device_id={"cell": lax.rem(cell + step, strips), "lev": lev},
            device_id_type=MESH,
        )
        greeted += 1
    for step in range(1, groups // 2):
        pl.semaphore_signal(
            barrier,
            inc=1,
            device_id={"cell": cell, "lev": lax.rem(lev + 2 * step, groups)},
            device_id_type=MESH,
        )
        greeted += 1
    pl.semaphore_signal(barrier, inc=1, device_id={"cell": cell, "lev": partner}, device_id_type=MESH)
    greeted += 1

    operands = [
        pltpu.make_async_copy(source, into, operand_sem.at[index])
        for index, (source, into) in enumerate(
            (
                (p_hbm, p_ref),
                (absorber_hbm, absorber_ref),
                (cross_hbm, cross_ref),
                (emission_hbm, emission_ref),
                (stream_hbm, stream_ref),
                (turn_hbm, turn_ref),
                (bracket_hbm, bracket_ref),
                (inflow_hbm, inflow_ref),
                (pattern_hbm, pattern_ref),
            )
        )
    ]
    for copy in operands:
        copy.start()
    fetch = pltpu.make_async_copy(rates_hbm, rates, rates_sem)
    fetch.start()

    def rows(x):
        return slice(x * NY, (x + 1) * NY)

    def spread(row):
        shape = (cell_count, cell_count)
        here = lax.broadcasted_iota(jnp.int32, shape, 0) == lax.broadcasted_iota(jnp.int32, shape, 1)
        column = jnp.sum(jnp.where(here, row, 0.0), axis=1, keepdims=True)
        return jnp.broadcast_to(column, (cell_count, LANES))

    def summed_layers(row):
        shape = (NY, cell_count)
        cell_y = lax.rem(lax.broadcasted_iota(jnp.int32, shape, 1), NY)
        here = lax.broadcasted_iota(jnp.int32, shape, 0) == cell_y
        column = jnp.sum(jnp.where(here, row, 0.0), axis=1, keepdims=True)
        return jnp.broadcast_to(column, (NY, LANES))

    def lanes(block):
        return pl.ds(pl.multiple_of(block * LANES, LANES), LANES)

    def turn_of(index):
        return lax.rem(pos + 1 + index, half)

    def own_slot(part, who, share):
        return gathered[part].at[pl.ds(who * blocks + share * piece, piece)]

    def gather_copy(part, to, source, send_sem, share):
        return pltpu.make_async_remote_copy(
            src_ref=own_slot(part, source, share),
            dst_ref=own_slot(part, source, share),
            send_sem=send_sem.at[share],
            recv_sem=gather_recv.at[part, source, share],
            device_id={"cell": cell, "lev": to},
            device_id_type=MESH,
        )

    def partner_copy(part, who):
        return pltpu.make_async_remote_copy(
            src_ref=gathered[part].at[pl.ds(who * blocks, blocks)],
            dst_ref=gathered[part].at[pl.ds(who * blocks, blocks)],
            send_sem=partner_send.at[part],
            recv_sem=partner_recv.at[part],
            device_id={"cell": cell, "lev": partner},
            device_id_type=MESH,
        )

    def halo_copy(part):
        return pltpu.make_async_remote_copy(
            src_ref=gathered[part].at[pl.ds(lev * blocks, blocks), pl.ds(cell_count - NY, NY)],
            dst_ref=halo.at[part],
            send_sem=halo_send.at[part],
            recv_sem=halo_recv.at[part],
            device_id={"cell": lax.rem(cell + 1, strips), "lev": lev},
            device_id_type=MESH,
        )

    def column_copy(step):
        to = lax.rem(cell + step, strips)
        return pltpu.make_async_remote_copy(
            src_ref=columns.at[cell],
            dst_ref=columns.at[cell],
            send_sem=column_send.at[step],
            recv_sem=column_recv.at[step],
            device_id={"cell": to, "lev": lev},
            device_id_type=MESH,
        )

    def near_copy(part, share, who):
        return pltpu.make_async_remote_copy(
            src_ref=out_one.at[part, share],
            dst_ref=in_near.at[part, who],
            send_sem=near_send.at[part, share],
            recv_sem=near_recv.at[part, who],
            device_id={"cell": base + share, "lev": lev},
            device_id_type=MESH,
        )

    def far_copy(part, share, who):
        return pltpu.make_async_remote_copy(
            src_ref=out_one.at[part, share, pl.ds(piece * side, piece)],
            dst_ref=in_far.at[part, who],
            send_sem=far_send.at[part, share],
            recv_sem=far_recv.at[part, who],
            device_id={"cell": other + share, "lev": lev},
            device_id_type=MESH,
        )

    def two_copy(part, to, who):
        return pltpu.make_async_remote_copy(
            src_ref=out_two.at[part, to],
            dst_ref=in_two.at[part, who],
            send_sem=two_send.at[part, to],
            recv_sem=two_recv.at[part, who],
            device_id={"cell": base + to, "lev": lev},
            device_id_type=MESH,
        )

    def emitted_of(value, block):
        return value * emission_ref[pl.ds(block, 1), :]

    def put(ref, part, index, downs, ups):
        means = []
        for place, value in enumerate(downs + ups):
            mean = jnp.mean(value, axis=0, keepdims=True).astype(jnp.bfloat16).astype(jnp.float32)
            ref[part, index, place + place // piece] = (value - mean).astype(jnp.bfloat16)
            means.append(mean)
        if len(means) < NY:
            means.append(jnp.zeros((NY - len(means), LANES), jnp.float32))
        ref[part, index, piece] = jnp.concatenate(means, axis=0).astype(jnp.bfloat16)

    def get(ref, part, index, b):
        means = ref[part, index, piece].astype(jnp.float32)
        return tuple(
            ref[part, index, place + place // piece].astype(jnp.float32) + means[place : place + 1]
            for place in (b, piece + b)
        )

    def is_first():
        return lax.broadcasted_iota(jnp.int32, (NY, LANES), 0) == 0

    def put_sums(part, share, downs, ups):
        for place, value in enumerate(downs + ups):
            first = value[:1].astype(jnp.bfloat16).astype(jnp.float32)
            out_one[part, share, place] = jnp.where(is_first(), value, value - first).astype(
                jnp.bfloat16
            )

    def restored(tile):
        value = tile.astype(jnp.float32)
        return jnp.where(is_first(), value, value + value[:1])

    def lower(part, block, value):
        gathered[part][lev * blocks + block] = value.astype(jnp.bfloat16)

    def summarize(part, share, values):
        downs, ups = [], []
        for b in range(piece):
            block = share * piece + b
            through = [passing[block, rows(x), :] for x in range(layers)]
            emit = [emitted_of(values[b][x], block) for x in range(layers)]
            down, up = emit[0], emit[-1]
            for x in range(1, layers):
                down = through[x] * down + emit[x]
                up = through[layers - 1 - x] * up + emit[layers - 1 - x]
            downs.append(down)
            ups.append(up)
        put_sums(part, share, downs, ups)

    def send_summary(part, share):
        far_copy(part, share, slot).start()

        @pl.when(share != pos)
        def _():
            near_copy(part, share, pos).start()

        @pl.when(share == pos)
        def _():
            in_near[part, pos] = out_one[part, pos]

    def load_start(block):
        return [p_ref[rows(x), lanes(block)] for x in range(layers)]

    def load_middle(block):
        return [middle[block, rows(x), :] for x in range(layers)]

    def start_gather(part, share):
        for step in range(1, groups // 2):
            to = lax.rem(lev + 2 * step, groups)
            gather_copy(part, to, lev, gather_send.at[part, step], share).start()

    def start_halo(part):
        @pl.when(cell < strips - 1)
        def _():
            halo_copy(part).start()

    def lower_start(block, _):
        lower(0, block, p_ref[:, lanes(block)])
        return 0

    def summarize_start(index, _):
        share = turn_of(index)
        values = []
        for b in range(piece):
            block = share * piece + b
            passing[block] = jnp.exp(-(coef[0] * cross_ref[pl.ds(block, 1), :]))
            values.append(load_start(block))
        summarize(0, share, values)
        return 0

    for copy in operands[:4]:
        copy.wait()
    lax.fori_loop(0, blocks, lower_start, 0, unroll=4)
    columns[cell] = absorber_ref[...]
    coef[0] = spread(absorber_ref[...])
    lax.fori_loop(0, half, summarize_start, 0)
    pl.semaphore_wait(barrier, greeted)
    for step in range(1, strips):
        column_copy(step).start()
    start_gather(0, turn_of(0))
    for index in range(half):
        send_summary(0, turn_of(index))
    start_gather(0, turn_of(1))
    for index in range(2, half):
        start_gather(0, turn_of(index))
    partner_copy(0, lev).start()
    for copy in operands[4:]:
        copy.wait()
    start_halo(0)
    coef[1] = spread(stream_ref[...])
    coef[2] = spread(turn_ref[...])
    coef[3] = spread(bracket_ref[...].astype(jnp.float32))

    @pl.when(cell == 0)
    def _():
        for part in range(2):
            for block in range(blocks):
                halo[part, block] = inflow_ref[:, block * LANES : (block + 1) * LANES].astype(
                    jnp.bfloat16
                )

    fetch.wait()

    def turn_tables(row, _):
        for bracket in range(brackets):
            for k in range(nonzero):
                rates[bracket, row, k] = rates[bracket, row, k].T
        return 0

    lax.fori_loop(0, blocks, turn_tables, 0, unroll=2)
    for step in range(1, strips):
        column_copy(step).wait()

    def share_block(index, _):
        near = summed_layers(columns[base + index])
        far = summed_layers(columns[other + index + (1 - side) * (half - 1 - 2 * index)])
        for b in range(piece):
            cross = cross_ref[pl.ds(pos * piece + b, 1), :]
            near_pass[index, b] = jnp.exp(-(near * cross))
            far_pass[index, b] = jnp.exp(-(far * cross))
        return 0

    lax.fori_loop(0, half, share_block, 0)

    def enter(part):
        for index in range(half):
            far_copy(part, index, index).wait_recv()
        for step in range(1, half):
            near_copy(part, pos, lax.rem(pos + step, half)).wait_recv()
        below = [[] for _ in range(half)]
        above = [[] for _ in range(half)]
        for b in range(piece):
            beyond = jnp.zeros((NY, LANES), jnp.float32)
            for index in range(half):
                beyond = far_pass[index, b] * beyond + restored(in_far[part, index, b])
            parts = [
                (restored(in_near[part, index, b]), restored(in_near[part, index, piece + b]))
                for index in range(half)
            ]
            running = jnp.where(side == 1, beyond, 0.0)
            for index in range(half):
                below[index].append(running)
                running = near_pass[index, b] * running + parts[index][0]
            running = jnp.where(side == 0, beyond, 0.0)
            for index in reversed(range(half)):
                above[index].append(running)
                running = near_pass[index, b] * running + parts[index][1]
        for index in range(half):
            put(out_two, part, index, below[index], above[index])
        for step in range(1, half):
            two_copy(part, lax.rem(pos + step, half), pos).start()
        in_two[part, pos] = out_two[part, pos]

    def forward(part, share):
        for step in range(1, groups // 2):
            source = lax.rem(lev + 2 * step, groups)
            gather_copy(part, lev, source, gather_send.at[part, step], share).wait_recv()
            gather_copy(part, partner, source, forward_send.at[part, step], share).start()

    def all_gathered(part):
        partner_copy(part, partner).wait_recv()
        for index in range(half):
            for step in range(1, groups // 2):
                source = lax.rem(partner + 2 * step, groups)
                gather_copy(part, lev, source, gather_send.at[part, step], turn_of(index)).wait_recv()

    def rate_row(part, row):
        picked = jnp.concatenate(
            [gathered[part][pattern_ref[k, row]] for k in range(nonzero)], axis=1
        )
        table = jnp.concatenate(
            [
                jnp.concatenate([rates[bracket, row, k] for k in range(nonzero)], axis=0)
                for bracket in range(brackets)
            ],
            axis=1,
        )
        product = jnp.dot(picked, table, preferred_element_type=jnp.float32)
        kind = coef[3]
        summed = product[:, :LANES]
        for bracket in range(1, brackets):
            summed = jnp.where(
                kind == float(bracket),
                product[:, bracket * LANES : (bracket + 1) * LANES],
                summed,
            )
        return summed

    def finish_transfers(part):
        partner_copy(part, lev).wait_send()
        for index in range(half):
            for step in range(1, groups // 2):
                gather_copy(part, partner, lev, gather_send.at[part, step], index).wait_send()
                gather_copy(part, partner, lev, forward_send.at[part, step], index).wait_send()
            far_copy(part, index, slot).wait_send()
        for step in range(1, half):
            near_copy(part, lax.rem(pos + step, half), pos).wait_send()
            two_copy(part, lax.rem(pos + step, half), pos).wait_send()

        @pl.when(cell < strips - 1)
        def _():
            halo_copy(part).wait_send()

    def before_close(part):
        @pl.when(cell > 0)
        def _():
            halo_copy(part).wait_recv()

    def rates_of(part, share):
        return [rate_row(part, share * piece + b) for b in range(piece)]

    def tabulate(block, _):
        through = [passing[block, rows(x), :] for x in range(layers)]
        down, up = through[0], through[-1]
        for x in range(layers):
            back = layers - 1 - x
            if x > 0:
                down = through[x] * down
                up = through[back] * up
            from_below[block, rows(x), :] = (1.0 - through[x]) * down
            from_above[block, rows(back), :] = (1.0 - through[back]) * up
        return 0

    def prepare(part, load):
        def one_block(block, _):
            value = load(block)
            through = [passing[block, rows(x), :] for x in range(layers)]
            emit = [emitted_of(value[x], block) for x in range(layers)]
            downs, ups = [emit[0]], [emit[-1]]
            for x in range(1, layers):
                downs.append(through[x] * downs[-1] + emit[x])
                ups.insert(0, through[layers - 1 - x] * ups[0] + emit[layers - 1 - x])
            arrived = halo[part, block].astype(jnp.float32)
            entering = jnp.where(cell == 0, inflow_ref[:, lanes(block)], arrived)
            for x in range(layers):
                taken = (1.0 - through[x]) * (downs[x] + ups[x] - 2.0 * emit[x])
                upstream = entering if x == 0 else value[x - 1]
                before_y = pltpu.roll(value[x], 1, 0)
                after_y = pltpu.roll(value[x], NY - 1, 0)
                cross = coef[2, rows(x), :]
                carried = (
                    -coef[1, rows(x), :] * (value[x] - upstream)
                    - jnp.maximum(cross, 0.0) * (value[x] - before_y)
                    - jnp.minimum(cross, 0.0) * (after_y - value[x])
                )
                if part:
                    inside[block, rows(x), :] = taken
                known[block, rows(x), :] = value[x] + time_step * (taken + carried - emit[x])
            return 0

        lax.fori_loop(0, blocks, one_block, 0, unroll=2)

    def outside(part, share, b):
        block = share * piece + b
        down, up = get(in_two, part, share, b)
        return [
            from_below[block, rows(x), :] * down + from_above[block, rows(x), :] * up
            for x in range(layers)
        ]

    def exchange(part, load):
        early = half // 2 if part else half // 4
        for index in range(early):
            forward(part, turn_of(index))
        enter(part)
        for index in range(early, half - 1):
            forward(part, turn_of(index))
        before_close(part)
        prepare(part, load)
        forward(part, turn_of(half - 1))
        all_gathered(part)

    def arrived_two(part, share):
        @pl.when(share != pos)
        def _():
            two_copy(part, pos, share).wait_recv()

    lax.fori_loop(0, blocks, tabulate, 0)
    exchange(0, load_start)

    def close_first(share, sums):
        arrived_two(0, share)
        values = []
        for b in range(piece):
            block = share * piece + b
            added = outside(0, share, b)
            renewed = [
                known[block, rows(x), :] + time_step * (sums[b][rows(x)] + added[x])
                for x in range(layers)
            ]
            for x in range(layers):
                middle[block, rows(x), :] = renewed[x]
            lower(1, block, jnp.concatenate(renewed, axis=0))
            values.append(renewed)
        start_gather(1, share)
        summarize(1, share, values)
        send_summary(1, share)

    ready = [rates_of(0, turn_of(index)) for index in range(min(2, half))]
    for index in range(half):
        if index + 2 < half:
            ready.append(rates_of(0, turn_of(index + 2)))
        close_first(turn_of(index), ready[index])
    partner_copy(1, lev).start()
    start_halo(1)
    finish_transfers(0)
    exchange(1, load_middle)
    finish_transfers(1)

    def close_second(share, sums):
        arrived_two(1, share)
        for b in range(piece):
            block = share * piece + b
            start = load_start(block)
            added = outside(1, share, b)
            for x in range(layers):
                gained_ref[rows(x), lanes(block)] = 2.0 * (inside[block, rows(x), :] + added[x])
                renewed = known[block, rows(x), :] + time_step * (sums[b][rows(x)] + added[x])
                advanced_ref[rows(x), lanes(block)] = start[x] + renewed

    def own_first(index):
        return lax.rem(pos + index, half)

    ready = [rates_of(1, own_first(index)) for index in range(min(2, half))]
    for index in range(half):
        if index + 2 < half:
            ready.append(rates_of(1, own_first(index + 2)))
        close_second(own_first(index), ready[index])


def fused(
    strips,
    groups,
    populations,
    rate_blocks,
    pattern,
    bracket,
    cross_section,
    emission,
    absorber,
    stream_speed,
    cross_speed,
    inflow,
):
    cell_count, level_count = populations.shape
    blocks = level_count // LANES
    half = strips // 2
    piece = blocks // half
    layers_shape = (blocks, cell_count, LANES)
    message = (2 * piece + 1, NY, LANES)
    vmem = pl.BlockSpec(memory_space=pltpu.VMEM)
    dma = pltpu.SemaphoreType.DMA
    operands = [
        pattern.T,
        populations,
        rate_blocks,
        bracket.reshape(1, -1),
        absorber.reshape(1, -1),
        stream_speed.reshape(1, -1),
        cross_speed.reshape(1, -1),
        cross_section.reshape(blocks, LANES),
        emission.reshape(blocks, LANES),
        inflow,
    ]
    held = [pltpu.VMEM(value.shape, value.dtype) for value in operands]
    held[0] = pltpu.SMEM(operands[0].shape, operands[0].dtype)
    del held[2]
    return pl.pallas_call(
        functools.partial(fused_kernel, strips, groups),
        out_shape=[pltpu.VMEM((cell_count, level_count), jnp.float32)] * 2,
        in_specs=[pl.BlockSpec(memory_space=pltpu.HBM)] * len(operands),
        out_specs=[vmem, vmem],
        scratch_shapes=held
        + [
            pltpu.VMEM(rate_blocks.shape, rate_blocks.dtype),
            pltpu.VMEM((4, cell_count, LANES), jnp.float32),
            pltpu.VMEM(layers_shape, jnp.float32),
            pltpu.VMEM(layers_shape, jnp.float32),
            pltpu.VMEM(layers_shape, jnp.float32),
            pltpu.VMEM(layers_shape, jnp.float32),
            pltpu.VMEM(layers_shape, jnp.float32),
            pltpu.VMEM(layers_shape, jnp.float32),
            pltpu.VMEM((groups * blocks, cell_count, LANES), jnp.bfloat16),
            pltpu.VMEM((groups * blocks, cell_count, LANES), jnp.bfloat16),
            pltpu.VMEM((2, blocks, NY, LANES), jnp.bfloat16),
            pltpu.VMEM((strips, 1, cell_count), jnp.float32),
            pltpu.VMEM((half, piece, NY, LANES), jnp.float32),
            pltpu.VMEM((half, piece, NY, LANES), jnp.float32),
            pltpu.VMEM((2, half, 2 * piece, NY, LANES), jnp.bfloat16),
            pltpu.VMEM((2, half, 2 * piece, NY, LANES), jnp.bfloat16),
            pltpu.VMEM((2, half, piece, NY, LANES), jnp.bfloat16),
            pltpu.VMEM((2, half) + message, jnp.bfloat16),
            pltpu.VMEM((2, half) + message, jnp.bfloat16),
            dma(()),
            dma((len(held),)),
            dma((2, groups, half)),
            dma((2, groups, half)),
            dma((2, groups, half)),
            dma((2,)),
            dma((2,)),
            dma((2,)),
            dma((2,)),
            dma((strips,)),
            dma((strips,)),
            dma((2, half)),
            dma((2, half)),
            dma((2, half)),
            dma((2, half)),
            dma((2, half)),
            dma((2, half)),
        ],
        compiler_params=pltpu.CompilerParams(
            collective_id=0, has_side_effects=True, vmem_limit_bytes=24 * 1024 * 1024
        ),
    )(*[pltpu.with_memory_space_constraint(value, pltpu.HBM) for value in operands])


def shortened(value):

    def short(part):
        return part.astype(jnp.bfloat16) if part.dtype == jnp.float32 else part

    return jax.tree.map(short, value)


def shifted(value, axis, by):
    peers = lax.axis_size(axis)
    pairs = [(i, i + by) for i in range(peers) if 0 <= i + by < peers]
    return lax.ppermute(value, axis, pairs)


def affine(earlier, later):
    return (earlier[0] * later[0], later[0] * earlier[1] + later[1])


def rate_term(populations, rate_blocks, pattern, bracket):
    lowered = populations.astype(jnp.bfloat16)
    gathered = lax.all_gather(lowered, "lev", axis=1, tiled=True)
    cell_count = gathered.shape[0]
    brackets, rows, nonzero, block_size = rate_blocks.shape[:4]
    by_block = jnp.swapaxes(gathered.reshape(cell_count, -1, block_size), 0, 1)

    def one_row(row):
        summed = jnp.zeros((cell_count, block_size), jnp.float32)
        for bracket_id in range(brackets):
            product = jnp.zeros((cell_count, block_size), jnp.float32)
            for k in range(nonzero):
                column = lax.dynamic_index_in_dim(by_block, pattern[row, k], 0, keepdims=False)
                table = lax.dynamic_index_in_dim(rate_blocks[bracket_id], row, 0, keepdims=False)[k]
                product += jnp.einsum("cj,ij->ci", column, table, preferred_element_type=jnp.float32)
            summed = jnp.where((bracket == bracket_id)[:, None], product, summed)
        return summed

    stacked = lax.map(one_row, jnp.arange(rows, dtype=jnp.int32))
    return jnp.transpose(stacked, (1, 0, 2)).reshape(cell_count, -1)


def entering(received):
    start = jnp.zeros(received.shape[2:], jnp.float32)

    def advance(running, layer_in):
        return (layer_in[0] * running + layer_in[1], running)

    _, from_below = lax.scan(advance, start, (received[:, 0], received[:, 1]))
    _, from_above = lax.scan(advance, start, (received[:, 2], received[:, 3]), reverse=True)
    both_sides = jnp.stack([from_below, from_above], axis=1)
    return lax.all_to_all(both_sides, "cell", split_axis=0, concat_axis=3, tiled=True)


def radiation(populations, emission, cross_section, absorber):
    cell_count, level_count = populations.shape
    strips = cell_count // NY
    emitted = populations * emission[None, :]
    transmit = jnp.exp(-(absorber[:, None] * cross_section[None, :]))
    layered_pass = transmit.reshape(strips, NY, level_count)
    layered_emit = emitted.reshape(strips, NY, level_count)
    passed_down, local_down = lax.associative_scan(affine, (layered_pass, layered_emit), axis=0)
    passed_up, local_up = lax.associative_scan(
        affine, (layered_pass, layered_emit), reverse=True, axis=0
    )
    summary = jnp.stack([passed_down[-1], local_down[-1], passed_up[0], local_up[0]])[None]
    returned = entering(lax.all_to_all(summary, "cell", split_axis=3, concat_axis=0, tiled=True))
    enter_down = returned[0, 0]
    enter_up = returned[0, 1]
    downward = local_down + passed_down * enter_down[None]
    upward = local_up + passed_up * enter_up[None]
    absorbed = (1.0 - layered_pass) * (downward + upward - 2.0 * layered_emit)
    return (emitted, absorbed.reshape(cell_count, level_count))


def advection(populations, inflow, stream_speed, cross_speed):
    cell_count, level_count = populations.shape
    layered = populations.reshape(cell_count // NY, NY, level_count)
    arrived = shifted(shortened(layered[-1]), "cell", 1)
    boundary = jnp.where(lax.axis_index("cell") == 0, inflow, arrived)
    upstream = jnp.concatenate([boundary[None], layered[:-1]], axis=0)
    before_y = jnp.roll(layered, 1, axis=1)
    after_y = jnp.roll(layered, -1, axis=1)
    along_x = stream_speed.reshape(-1, NY, 1)
    along_y = cross_speed.reshape(-1, NY, 1)
    flux_sum = (
        -along_x * (layered - upstream)
        - jnp.maximum(along_y, 0.0) * (layered - before_y)
        - jnp.minimum(along_y, 0.0) * (after_y - layered)
    )
    return flux_sum.reshape(cell_count, level_count)


def tendency(
    populations,
    rate_blocks,
    pattern,
    bracket,
    cross_section,
    emission,
    absorber,
    stream_speed,
    cross_speed,
    inflow,
):
    rates_part = rate_term(populations, rate_blocks, pattern, bracket)
    emitted, absorbed = radiation(populations, emission, cross_section, absorber)
    carried = advection(populations, inflow, stream_speed, cross_speed)
    return (rates_part - emitted + absorbed + carried, absorbed)


def local(
    populations,
    rate_blocks,
    pattern,
    bracket,
    cross_section,
    emission,
    absorber,
    stream_speed,
    cross_speed,
    inflow,
):
    strips, groups = lax.axis_size("cell"), lax.axis_size("lev")
    cell_count, level_count = populations.shape
    if (
        groups % 2 == 0
        and strips % 2 == 0
        and cell_count % NY == 0
        and level_count % (strips // 2 * LANES) == 0
        and rate_blocks.shape[3] == LANES
        and 4 * level_count <= strips * LANES * NY
    ):
        advanced, gained = (
            fused(
                strips,
                groups,
                populations,
                rate_blocks,
                pattern,
                bracket,
                cross_section,
                emission,
                absorber,
                stream_speed,
                cross_speed,
                inflow,
            )
        )
        return (0.5 * advanced, 0.5 * gained)
    first_rate, _ = tendency(
        populations,
        rate_blocks,
        pattern,
        bracket,
        cross_section,
        emission,
        absorber,
        stream_speed,
        cross_speed,
        inflow,
    )
    middle = populations + time_step * first_rate
    second, absorption = tendency(
        middle,
        rate_blocks,
        pattern,
        bracket,
        cross_section,
        emission,
        absorber,
        stream_speed,
        cross_speed,
        inflow,
    )
    updated = 0.5 * (populations + middle + time_step * second)
    return (updated, absorption)


def solution(mesh):
    in_specs = (
        P("cell", "lev"),
        P(None, "lev", None, None, None),
        P("lev", None),
        P("cell"),
        P("lev"),
        P("lev"),
        P("cell"),
        P("cell"),
        P("cell"),
        P(None, "lev"),
    )
    out_specs = (P("cell", "lev"), P("cell", "lev"))
    return jax.shard_map(local, mesh=mesh, in_specs=in_specs, out_specs=out_specs, check_vma=False)
```

```python
import functools

import jax
import jax.numpy as jnp
from jax import lax
from jax.experimental import pallas as pl
from jax.experimental.pallas import tpu as pltpu
from jax.sharding import PartitionSpec as P

NY = 16
LANES = 128

time_step = 0.25

MESH = pl.DeviceIdType.MESH


def fused_kernel(
    strips,
    groups,
    pattern_hbm,
    p_hbm,
    rates_hbm,
    bracket_hbm,
    absorber_hbm,
    stream_hbm,
    turn_hbm,
    cross_hbm,
    emission_hbm,
    inflow_hbm,
    advanced_ref,
    gained_ref,
    pattern_ref,
    p_ref,
    bracket_ref,
    absorber_ref,
    stream_ref,
    turn_ref,
    cross_ref,
    emission_ref,
    inflow_ref,
    rates,
    coef,
    passing,
    middle,
    known,
    inside,
    from_below,
    from_above,
    gathered_first,
    gathered_second,
    halo,
    columns,
    near_pass,
    far_pass,
    out_one,
    in_near,
    in_far,
    out_two,
    in_two,
    rates_sem,
    operand_sem,
    gather_send,
    gather_recv,
    forward_send,
    partner_send,
    partner_recv,
    halo_send,
    halo_recv,
    column_send,
    column_recv,
    near_send,
    near_recv,
    far_send,
    far_recv,
    two_send,
    two_recv,
):
    cell = lax.axis_index("cell")
    lev = lax.axis_index("lev")
    gathered = (gathered_first, gathered_second)
    cell_count = p_ref.shape[0]
    layers = cell_count // NY
    blocks = p_ref.shape[1] // LANES
    half = strips // 2
    piece = blocks // half
    brackets, _, nonzero = rates_hbm.shape[:3]
    partner = lev + 1 - 2 * lax.rem(lev, 2)
    side = cell // half
    pos = lax.rem(cell, half)
    base = side * half
    other = (1 - side) * half
    slot = pos + side * (half - 1 - 2 * pos)

    barrier = pltpu.get_barrier_semaphore()
    greeted = 0
    for step in range(1, strips):
        pl.semaphore_signal(
            barrier,
            inc=1,
            device_id={"cell": lax.rem(cell + step, strips), "lev": lev},
            device_id_type=MESH,
        )
        greeted += 1
    for step in range(1, groups // 2):
        pl.semaphore_signal(
            barrier,
            inc=1,
            device_id={"cell": cell, "lev": lax.rem(lev + 2 * step, groups)},
            device_id_type=MESH,
        )
        greeted += 1
    pl.semaphore_signal(barrier, inc=1, device_id={"cell": cell, "lev": partner}, device_id_type=MESH)
    greeted += 1

    operands = [
        pltpu.make_async_copy(source, into, operand_sem.at[index])
        for index, (source, into) in enumerate(
            (
                (p_hbm, p_ref),
                (absorber_hbm, absorber_ref),
                (cross_hbm, cross_ref),
                (emission_hbm, emission_ref),
                (stream_hbm, stream_ref),
                (turn_hbm, turn_ref),
                (bracket_hbm, bracket_ref),
                (inflow_hbm, inflow_ref),
                (pattern_hbm, pattern_ref),
            )
        )
    ]
    for copy in operands:
        copy.start()
    fetch = pltpu.make_async_copy(rates_hbm, rates, rates_sem)
    fetch.start()

    def rows(x):
        return slice(x * NY, (x + 1) * NY)

    def spread(row):
        shape = (cell_count, cell_count)
        here = lax.broadcasted_iota(jnp.int32, shape, 0) == lax.broadcasted_iota(jnp.int32, shape, 1)
        column = jnp.sum(jnp.where(here, row, 0.0), axis=1, keepdims=True)
        return jnp.broadcast_to(column, (cell_count, LANES))

    def summed_layers(row):
        shape = (NY, cell_count)
        cell_y = lax.rem(lax.broadcasted_iota(jnp.int32, shape, 1), NY)
        here = lax.broadcasted_iota(jnp.int32, shape, 0) == cell_y
        column = jnp.sum(jnp.where(here, row, 0.0), axis=1, keepdims=True)
        return jnp.broadcast_to(column, (NY, LANES))

    def lanes(block):
        return pl.ds(pl.multiple_of(block * LANES, LANES), LANES)

    def turn_of(index):
        return lax.rem(pos + 1 + index, half)

    def own_slot(part, who, share):
        return gathered[part].at[pl.ds(who * blocks + share * piece, piece)]

    def gather_copy(part, to, source, send_sem, share):
        return pltpu.make_async_remote_copy(
            src_ref=own_slot(part, source, share),
            dst_ref=own_slot(part, source, share),
            send_sem=send_sem.at[share],
            recv_sem=gather_recv.at[part, source, share],
            device_id={"cell": cell, "lev": to},
            device_id_type=MESH,
        )

    def partner_copy(part, who):
        return pltpu.make_async_remote_copy(
            src_ref=gathered[part].at[pl.ds(who * blocks, blocks)],
            dst_ref=gathered[part].at[pl.ds(who * blocks, blocks)],
            send_sem=partner_send.at[part],
            recv_sem=partner_recv.at[part],
            device_id={"cell": cell, "lev": partner},
            device_id_type=MESH,
        )

    def halo_copy(part):
        return pltpu.make_async_remote_copy(
            src_ref=gathered[part].at[pl.ds(lev * blocks, blocks), pl.ds(cell_count - NY, NY)],
            dst_ref=halo.at[part],
            send_sem=halo_send.at[part],
            recv_sem=halo_recv.at[part],
            device_id={"cell": lax.rem(cell + 1, strips), "lev": lev},
            device_id_type=MESH,
        )

    def column_copy(step):
        to = lax.rem(cell + step, strips)
        return pltpu.make_async_remote_copy(
            src_ref=columns.at[cell],
            dst_ref=columns.at[cell],
            send_sem=column_send.at[step],
            recv_sem=column_recv.at[step],
            device_id={"cell": to, "lev": lev},
            device_id_type=MESH,
        )

    def near_copy(part, share, who):
        return pltpu.make_async_remote_copy(
            src_ref=out_one.at[part, share],
            dst_ref=in_near.at[part, who],
            send_sem=near_send.at[part, share],
            recv_sem=near_recv.at[part, who],
            device_id={"cell": base + share, "lev": lev},
            device_id_type=MESH,
        )

    def far_copy(part, share, who):
        return pltpu.make_async_remote_copy(
            src_ref=out_one.at[part, share, pl.ds(piece * side, piece)],
            dst_ref=in_far.at[part, who],
            send_sem=far_send.at[part, share],
            recv_sem=far_recv.at[part, who],
            device_id={"cell": other + share, "lev": lev},
            device_id_type=MESH,
        )

    def two_copy(part, to, who):
        return pltpu.make_async_remote_copy(
            src_ref=out_two.at[part, to],
            dst_ref=in_two.at[part, who],
            send_sem=two_send.at[part, to],
            recv_sem=two_recv.at[part, who],
            device_id={"cell": base + to, "lev": lev},
            device_id_type=MESH,
        )

    def emitted_of(value, block):
        return value * emission_ref[pl.ds(block, 1), :]

    def put(ref, part, index, downs, ups):
        means = []
        for place, value in enumerate(downs + ups):
            mean = jnp.mean(value, axis=0, keepdims=True).astype(jnp.bfloat16).astype(jnp.float32)
            ref[part, index, place + place // piece] = (value - mean).astype(jnp.bfloat16)
            means.append(mean)
        if len(means) < NY:
            means.append(jnp.zeros((NY - len(means), LANES), jnp.float32))
        ref[part, index, piece] = jnp.concatenate(means, axis=0).astype(jnp.bfloat16)

    def get(ref, part, index, b):
        means = ref[part, index, piece].astype(jnp.float32)
        return tuple(
            ref[part, index, place + place // piece].astype(jnp.float32) + means[place : place + 1]
            for place in (b, piece + b)
        )

    def is_first():
        return lax.broadcasted_iota(jnp.int32, (NY, LANES), 0) == 0

    def put_sums(part, share, downs, ups):
        for place, value in enumerate(downs + ups):
            first = value[:1].astype(jnp.bfloat16).astype(jnp.float32)
            out_one[part, share, place] = jnp.where(is_first(), value, value - first).astype(
                jnp.bfloat16
            )

    def restored(tile):
        value = tile.astype(jnp.float32)
        return jnp.where(is_first(), value, value + value[:1])

    def lower(part, block, value):
        gathered[part][lev * blocks + block] = value.astype(jnp.bfloat16)

    def summarize(part, share, values):
        downs, ups = [], []
        for b in range(piece):
            block = share * piece + b
            through = [passing[block, rows(x), :] for x in range(layers)]
            emit = [emitted_of(values[b][x], block) for x in range(layers)]
            down, up = emit[0], emit[-1]
            for x in range(1, layers):
                down = through[x] * down + emit[x]
                up = through[layers - 1 - x] * up + emit[layers - 1 - x]
            downs.append(down)
            ups.append(up)
        put_sums(part, share, downs, ups)

    def send_summary(part, share):
        far_copy(part, share, slot).start()

        @pl.when(share != pos)
        def _():
            near_copy(part, share, pos).start()

        @pl.when(share == pos)
        def _():
            in_near[part, pos] = out_one[part, pos]

    def load_start(block):
        return [p_ref[rows(x), lanes(block)] for x in range(layers)]

    def load_middle(block):
        return [middle[block, rows(x), :] for x in range(layers)]

    def start_gather(part, share):
        for step in range(1, groups // 2):
            to = lax.rem(lev + 2 * step, groups)
            gather_copy(part, to, lev, gather_send.at[part, step], share).start()

    def start_halo(part):
        @pl.when(cell < strips - 1)
        def _():
            halo_copy(part).start()

    def lower_start(block, _):
        lower(0, block, p_ref[:, lanes(block)])
        return 0

    def summarize_start(index, _):
        share = turn_of(index)
        values = []
        for b in range(piece):
            block = share * piece + b
            passing[block] = jnp.exp(-(coef[0] * cross_ref[pl.ds(block, 1), :]))
            values.append(load_start(block))
        summarize(0, share, values)
        return 0

    for copy in operands[:4]:
        copy.wait()
    lax.fori_loop(0, blocks, lower_start, 0, unroll=4)
    columns[cell] = absorber_ref[...]
    coef[0] = spread(absorber_ref[...])
    lax.fori_loop(0, half, summarize_start, 0)
    pl.semaphore_wait(barrier, greeted)
    start_gather(0, turn_of(0))
    for step in range(1, strips):
        column_copy(step).start()
    start_gather(0, turn_of(1))
    for index in range(half):
        send_summary(0, turn_of(index))
    for index in range(2, half):
        start_gather(0, turn_of(index))
    partner_copy(0, lev).start()
    for copy in operands[4:]:
        copy.wait()
    start_halo(0)
    coef[1] = spread(stream_ref[...])
    coef[2] = spread(turn_ref[...])
    coef[3] = spread(bracket_ref[...].astype(jnp.float32))

    @pl.when(cell == 0)
    def _():
        for part in range(2):
            for block in range(blocks):
                halo[part, block] = inflow_ref[:, block * LANES : (block + 1) * LANES].astype(
                    jnp.bfloat16
                )

    fetch.wait()

    def turn_tables(row, _):
        for bracket in range(brackets):
            for k in range(nonzero):
                rates[bracket, row, k] = rates[bracket, row, k].T
        return 0

    lax.fori_loop(0, blocks, turn_tables, 0, unroll=2)
    for step in range(1, strips):
        column_copy(step).wait()

    def share_block(index, _):
        near = summed_layers(columns[base + index])
        far = summed_layers(columns[other + index + (1 - side) * (half - 1 - 2 * index)])
        for b in range(piece):
            cross = cross_ref[pl.ds(pos * piece + b, 1), :]
            near_pass[index, b] = jnp.exp(-(near * cross))
            far_pass[index, b] = jnp.exp(-(far * cross))
        return 0

    lax.fori_loop(0, half, share_block, 0)

    def enter(part):
        for index in range(half):
            far_copy(part, index, index).wait_recv()
        for step in range(1, half):
            near_copy(part, pos, lax.rem(pos + step, half)).wait_recv()
        below = [[] for _ in range(half)]
        above = [[] for _ in range(half)]
        for b in range(piece):
            beyond = jnp.zeros((NY, LANES), jnp.float32)
            for index in range(half):
                beyond = far_pass[index, b] * beyond + restored(in_far[part, index, b])
            parts = [
                (restored(in_near[part, index, b]), restored(in_near[part, index, piece + b]))
                for index in range(half)
            ]
            running = jnp.where(side == 1, beyond, 0.0)
            for index in range(half):
                below[index].append(running)
                running = near_pass[index, b] * running + parts[index][0]
            running = jnp.where(side == 0, beyond, 0.0)
            for index in reversed(range(half)):
                above[index].append(running)
                running = near_pass[index, b] * running + parts[index][1]
        for index in range(half):
            put(out_two, part, index, below[index], above[index])
        for step in range(1, half):
            two_copy(part, lax.rem(pos + step, half), pos).start()
        in_two[part, pos] = out_two[part, pos]

    def forward(part, share):
        for step in range(1, groups // 2):
            source = lax.rem(lev + 2 * step, groups)
            gather_copy(part, lev, source, gather_send.at[part, step], share).wait_recv()
            gather_copy(part, partner, source, forward_send.at[part, step], share).start()

    def all_gathered(part):
        partner_copy(part, partner).wait_recv()
        for index in range(half):
            for step in range(1, groups // 2):
                source = lax.rem(partner + 2 * step, groups)
                gather_copy(part, lev, source, gather_send.at[part, step], turn_of(index)).wait_recv()

    def rate_row(part, row):
        picked = jnp.concatenate(
            [gathered[part][pattern_ref[k, row]] for k in range(nonzero)], axis=1
        )
        table = jnp.concatenate(
            [
                jnp.concatenate([rates[bracket, row, k] for k in range(nonzero)], axis=0)
                for bracket in range(brackets)
            ],
            axis=1,
        )
        product = jnp.dot(picked, table, preferred_element_type=jnp.float32)
        kind = coef[3]
        summed = product[:, :LANES]
        for bracket in range(1, brackets):
            summed = jnp.where(
                kind == float(bracket),
                product[:, bracket * LANES : (bracket + 1) * LANES],
                summed,
            )
        return summed

    def finish_transfers(part):
        partner_copy(part, lev).wait_send()
        for index in range(half):
            for step in range(1, groups // 2):
                gather_copy(part, partner, lev, gather_send.at[part, step], index).wait_send()
                gather_copy(part, partner, lev, forward_send.at[part, step], index).wait_send()
            far_copy(part, index, slot).wait_send()
        for step in range(1, half):
            near_copy(part, lax.rem(pos + step, half), pos).wait_send()
            two_copy(part, lax.rem(pos + step, half), pos).wait_send()

        @pl.when(cell < strips - 1)
        def _():
            halo_copy(part).wait_send()

    def before_close(part):
        @pl.when(cell > 0)
        def _():
            halo_copy(part).wait_recv()

    def rates_of(part, share):
        return [rate_row(part, share * piece + b) for b in range(piece)]

    def tabulate(block, _):
        through = [passing[block, rows(x), :] for x in range(layers)]
        down, up = through[0], through[-1]
        for x in range(layers):
            back = layers - 1 - x
            if x > 0:
                down = through[x] * down
                up = through[back] * up
            from_below[block, rows(x), :] = (1.0 - through[x]) * down
            from_above[block, rows(back), :] = (1.0 - through[back]) * up
        return 0

    def prepare(part, load):
        def one_block(block, _):
            value = load(block)
            through = [passing[block, rows(x), :] for x in range(layers)]
            emit = [emitted_of(value[x], block) for x in range(layers)]
            downs, ups = [emit[0]], [emit[-1]]
            for x in range(1, layers):
                downs.append(through[x] * downs[-1] + emit[x])
                ups.insert(0, through[layers - 1 - x] * ups[0] + emit[layers - 1 - x])
            arrived = halo[part, block].astype(jnp.float32)
            entering = jnp.where(cell == 0, inflow_ref[:, lanes(block)], arrived)
            for x in range(layers):
                taken = (1.0 - through[x]) * (downs[x] + ups[x] - 2.0 * emit[x])
                upstream = entering if x == 0 else value[x - 1]
                before_y = pltpu.roll(value[x], 1, 0)
                after_y = pltpu.roll(value[x], NY - 1, 0)
                cross = coef[2, rows(x), :]
                carried = (
                    -coef[1, rows(x), :] * (value[x] - upstream)
                    - jnp.maximum(cross, 0.0) * (value[x] - before_y)
                    - jnp.minimum(cross, 0.0) * (after_y - value[x])
                )
                if part:
                    inside[block, rows(x), :] = taken
                known[block, rows(x), :] = value[x] + time_step * (taken + carried - emit[x])
            return 0

        lax.fori_loop(0, blocks, one_block, 0, unroll=2)

    def outside(part, share, b):
        block = share * piece + b
        down, up = get(in_two, part, share, b)
        return [
            from_below[block, rows(x), :] * down + from_above[block, rows(x), :] * up
            for x in range(layers)
        ]

    def exchange(part, load):
        early = half // 2 if part else half // 4
        for index in range(early):
            forward(part, turn_of(index))
        enter(part)
        for index in range(early, half - 1):
            forward(part, turn_of(index))
        before_close(part)
        prepare(part, load)
        forward(part, turn_of(half - 1))
        all_gathered(part)

    def arrived_two(part, share):
        @pl.when(share != pos)
        def _():
            two_copy(part, pos, share).wait_recv()

    lax.fori_loop(0, blocks, tabulate, 0)
    exchange(0, load_start)

    def close_first(share, sums):
        arrived_two(0, share)
        values = []
        for b in range(piece):
            block = share * piece + b
            added = outside(0, share, b)
            renewed = [
                known[block, rows(x), :] + time_step * (sums[b][rows(x)] + added[x])
                for x in range(layers)
            ]
            for x in range(layers):
                middle[block, rows(x), :] = renewed[x]
            lower(1, block, jnp.concatenate(renewed, axis=0))
            values.append(renewed)
        start_gather(1, share)
        summarize(1, share, values)
        send_summary(1, share)

    ready = [rates_of(0, turn_of(index)) for index in range(min(2, half))]
    for index in range(half):
        if index + 2 < half:
            ready.append(rates_of(0, turn_of(index + 2)))
        close_first(turn_of(index), ready[index])
    partner_copy(1, lev).start()
    start_halo(1)
    finish_transfers(0)
    exchange(1, load_middle)
    finish_transfers(1)

    def close_second(share, sums):
        arrived_two(1, share)
        for b in range(piece):
            block = share * piece + b
            start = load_start(block)
            added = outside(1, share, b)
            for x in range(layers):
                gained_ref[rows(x), lanes(block)] = inside[block, rows(x), :] + added[x]
                renewed = known[block, rows(x), :] + time_step * (sums[b][rows(x)] + added[x])
                advanced_ref[rows(x), lanes(block)] = 0.5 * (start[x] + renewed)

    def own_first(index):
        return lax.rem(pos + index, half)

    ready = [rates_of(1, own_first(index)) for index in range(min(2, half))]
    for index in range(half):
        if index + 2 < half:
            ready.append(rates_of(1, own_first(index + 2)))
        close_second(own_first(index), ready[index])


def deliver_kernel(first_ref, second_ref, first_hbm, second_hbm, sem):
    count = sem.shape[1]
    bite = first_ref.shape[0] // count
    copies = [
        pltpu.make_async_copy(
            source.at[pl.ds(index * bite, bite)], into.at[pl.ds(index * bite, bite)], sem.at[which, index]
        )
        for index in range(count)
        for which, (source, into) in enumerate(((first_ref, first_hbm), (second_ref, second_hbm)))
    ]
    for copy in copies:
        copy.start()
    for copy in copies:
        copy.wait()


def delivered(*values):
    value = values[0]
    count = 2 if value.shape[0] % (8 * 2) == 0 else 1
    return pl.pallas_call(
        deliver_kernel,
        out_shape=[jax.ShapeDtypeStruct(value.shape, value.dtype)] * len(values),
        in_specs=[pl.BlockSpec(memory_space=pltpu.VMEM)] * len(values),
        out_specs=[pl.BlockSpec(memory_space=pltpu.HBM)] * len(values),
        scratch_shapes=[pltpu.SemaphoreType.DMA((len(values), count))],
    )(*[pltpu.with_memory_space_constraint(value, pltpu.VMEM) for value in values])


def fused(
    strips,
    groups,
    populations,
    rate_blocks,
    pattern,
    bracket,
    cross_section,
    emission,
    absorber,
    stream_speed,
    cross_speed,
    inflow,
):
    cell_count, level_count = populations.shape
    blocks = level_count // LANES
    half = strips // 2
    piece = blocks // half
    layers_shape = (blocks, cell_count, LANES)
    message = (2 * piece + 1, NY, LANES)
    vmem = pl.BlockSpec(memory_space=pltpu.VMEM)
    dma = pltpu.SemaphoreType.DMA
    operands = [
        pattern.T,
        populations,
        rate_blocks,
        bracket.reshape(1, -1),
        absorber.reshape(1, -1),
        stream_speed.reshape(1, -1),
        cross_speed.reshape(1, -1),
        cross_section.reshape(blocks, LANES),
        emission.reshape(blocks, LANES),
        inflow,
    ]
    held = [pltpu.VMEM(value.shape, value.dtype) for value in operands]
    held[0] = pltpu.SMEM(operands[0].shape, operands[0].dtype)
    del held[2]
    return pl.pallas_call(
        functools.partial(fused_kernel, strips, groups),
        out_shape=[pltpu.VMEM((cell_count, level_count), jnp.float32)] * 2,
        in_specs=[pl.BlockSpec(memory_space=pltpu.HBM)] * len(operands),
        out_specs=[vmem, vmem],
        scratch_shapes=held
        + [
            pltpu.VMEM(rate_blocks.shape, rate_blocks.dtype),
            pltpu.VMEM((4, cell_count, LANES), jnp.float32),
            pltpu.VMEM(layers_shape, jnp.float32),
            pltpu.VMEM(layers_shape, jnp.float32),
            pltpu.VMEM(layers_shape, jnp.float32),
            pltpu.VMEM(layers_shape, jnp.float32),
            pltpu.VMEM(layers_shape, jnp.float32),
            pltpu.VMEM(layers_shape, jnp.float32),
            pltpu.VMEM((groups * blocks, cell_count, LANES), jnp.bfloat16),
            pltpu.VMEM((groups * blocks, cell_count, LANES), jnp.bfloat16),
            pltpu.VMEM((2, blocks, NY, LANES), jnp.bfloat16),
            pltpu.VMEM((strips, 1, cell_count), jnp.float32),
            pltpu.VMEM((half, piece, NY, LANES), jnp.float32),
            pltpu.VMEM((half, piece, NY, LANES), jnp.float32),
            pltpu.VMEM((2, half, 2 * piece, NY, LANES), jnp.bfloat16),
            pltpu.VMEM((2, half, 2 * piece, NY, LANES), jnp.bfloat16),
            pltpu.VMEM((2, half, piece, NY, LANES), jnp.bfloat16),
            pltpu.VMEM((2, half) + message, jnp.bfloat16),
            pltpu.VMEM((2, half) + message, jnp.bfloat16),
            dma(()),
            dma((len(held),)),
            dma((2, groups, half)),
            dma((2, groups, half)),
            dma((2, groups, half)),
            dma((2,)),
            dma((2,)),
            dma((2,)),
            dma((2,)),
            dma((strips,)),
            dma((strips,)),
            dma((2, half)),
            dma((2, half)),
            dma((2, half)),
            dma((2, half)),
            dma((2, half)),
            dma((2, half)),
        ],
        compiler_params=pltpu.CompilerParams(
            collective_id=0, has_side_effects=True, vmem_limit_bytes=24 * 1024 * 1024
        ),
    )(*[pltpu.with_memory_space_constraint(value, pltpu.HBM) for value in operands])


def shortened(value):

    def short(part):
        return part.astype(jnp.bfloat16) if part.dtype == jnp.float32 else part

    return jax.tree.map(short, value)


def shifted(value, axis, by):
    peers = lax.axis_size(axis)
    pairs = [(i, i + by) for i in range(peers) if 0 <= i + by < peers]
    return lax.ppermute(value, axis, pairs)


def affine(earlier, later):
    return (earlier[0] * later[0], later[0] * earlier[1] + later[1])


def rate_term(populations, rate_blocks, pattern, bracket):
    lowered = populations.astype(jnp.bfloat16)
    gathered = lax.all_gather(lowered, "lev", axis=1, tiled=True)
    cell_count = gathered.shape[0]
    brackets, rows, nonzero, block_size = rate_blocks.shape[:4]
    by_block = jnp.swapaxes(gathered.reshape(cell_count, -1, block_size), 0, 1)

    def one_row(row):
        summed = jnp.zeros((cell_count, block_size), jnp.float32)
        for bracket_id in range(brackets):
            product = jnp.zeros((cell_count, block_size), jnp.float32)
            for k in range(nonzero):
                column = lax.dynamic_index_in_dim(by_block, pattern[row, k], 0, keepdims=False)
                table = lax.dynamic_index_in_dim(rate_blocks[bracket_id], row, 0, keepdims=False)[k]
                product += jnp.einsum("cj,ij->ci", column, table, preferred_element_type=jnp.float32)
            summed = jnp.where((bracket == bracket_id)[:, None], product, summed)
        return summed

    stacked = lax.map(one_row, jnp.arange(rows, dtype=jnp.int32))
    return jnp.transpose(stacked, (1, 0, 2)).reshape(cell_count, -1)


def entering(received):
    start = jnp.zeros(received.shape[2:], jnp.float32)

    def advance(running, layer_in):
        return (layer_in[0] * running + layer_in[1], running)

    _, from_below = lax.scan(advance, start, (received[:, 0], received[:, 1]))
    _, from_above = lax.scan(advance, start, (received[:, 2], received[:, 3]), reverse=True)
    both_sides = jnp.stack([from_below, from_above], axis=1)
    return lax.all_to_all(both_sides, "cell", split_axis=0, concat_axis=3, tiled=True)


def radiation(populations, emission, cross_section, absorber):
    cell_count, level_count = populations.shape
    strips = cell_count // NY
    emitted = populations * emission[None, :]
    transmit = jnp.exp(-(absorber[:, None] * cross_section[None, :]))
    layered_pass = transmit.reshape(strips, NY, level_count)
    layered_emit = emitted.reshape(strips, NY, level_count)
    passed_down, local_down = lax.associative_scan(affine, (layered_pass, layered_emit), axis=0)
    passed_up, local_up = lax.associative_scan(
        affine, (layered_pass, layered_emit), reverse=True, axis=0
    )
    summary = jnp.stack([passed_down[-1], local_down[-1], passed_up[0], local_up[0]])[None]
    returned = entering(lax.all_to_all(summary, "cell", split_axis=3, concat_axis=0, tiled=True))
    enter_down = returned[0, 0]
    enter_up = returned[0, 1]
    downward = local_down + passed_down * enter_down[None]
    upward = local_up + passed_up * enter_up[None]
    absorbed = (1.0 - layered_pass) * (downward + upward - 2.0 * layered_emit)
    return (emitted, absorbed.reshape(cell_count, level_count))


def advection(populations, inflow, stream_speed, cross_speed):
    cell_count, level_count = populations.shape
    layered = populations.reshape(cell_count // NY, NY, level_count)
    arrived = shifted(shortened(layered[-1]), "cell", 1)
    boundary = jnp.where(lax.axis_index("cell") == 0, inflow, arrived)
    upstream = jnp.concatenate([boundary[None], layered[:-1]], axis=0)
    before_y = jnp.roll(layered, 1, axis=1)
    after_y = jnp.roll(layered, -1, axis=1)
    along_x = stream_speed.reshape(-1, NY, 1)
    along_y = cross_speed.reshape(-1, NY, 1)
    flux_sum = (
        -along_x * (layered - upstream)
        - jnp.maximum(along_y, 0.0) * (layered - before_y)
        - jnp.minimum(along_y, 0.0) * (after_y - layered)
    )
    return flux_sum.reshape(cell_count, level_count)


def tendency(
    populations,
    rate_blocks,
    pattern,
    bracket,
    cross_section,
    emission,
    absorber,
    stream_speed,
    cross_speed,
    inflow,
):
    rates_part = rate_term(populations, rate_blocks, pattern, bracket)
    emitted, absorbed = radiation(populations, emission, cross_section, absorber)
    carried = advection(populations, inflow, stream_speed, cross_speed)
    return (rates_part - emitted + absorbed + carried, absorbed)


def local(
    populations,
    rate_blocks,
    pattern,
    bracket,
    cross_section,
    emission,
    absorber,
    stream_speed,
    cross_speed,
    inflow,
):
    strips, groups = lax.axis_size("cell"), lax.axis_size("lev")
    cell_count, level_count = populations.shape
    if (
        groups % 2 == 0
        and strips % 2 == 0
        and cell_count % NY == 0
        and level_count % (strips // 2 * LANES) == 0
        and rate_blocks.shape[3] == LANES
        and 4 * level_count <= strips * LANES * NY
    ):
        advanced, gained = (
            fused(
                strips,
                groups,
                populations,
                rate_blocks,
                pattern,
                bracket,
                cross_section,
                emission,
                absorber,
                stream_speed,
                cross_speed,
                inflow,
            )
        )
        return delivered(advanced, gained)
    first_rate, _ = tendency(
        populations,
        rate_blocks,
        pattern,
        bracket,
        cross_section,
        emission,
        absorber,
        stream_speed,
        cross_speed,
        inflow,
    )
    middle = populations + time_step * first_rate
    second, absorption = tendency(
        middle,
        rate_blocks,
        pattern,
        bracket,
        cross_section,
        emission,
        absorber,
        stream_speed,
        cross_speed,
        inflow,
    )
    updated = 0.5 * (populations + middle + time_step * second)
    return (updated, absorption)


def solution(mesh):
    in_specs = (
        P("cell", "lev"),
        P(None, "lev", None, None, None),
        P("lev", None),
        P("cell"),
        P("lev"),
        P("lev"),
        P("cell"),
        P("cell"),
        P("cell"),
        P(None, "lev"),
    )
    out_specs = (P("cell", "lev"), P("cell", "lev"))
    return jax.shard_map(local, mesh=mesh, in_specs=in_specs, out_specs=out_specs, check_vma=False)
```
